256 devices in a mesh: row: 32 (over y, x, core), col: 8 (over z).
Axes of the slice: x: 4, y: 4, z: 8, core: 2. Of those that a mesh axis runs over, the one named last changes fastest.
Arguments:
- diag_block: float32 [512, 512], P(('row', 'col')), may hold values from 0 to 2, as said below
- panel_block: float32 [8192, 512], P('row', 'col'), may hold values from 0 to 1, as said below
- trailing: float32 [8192, 8192], P('row', 'col'), may hold values from 0 to 2, as said below
Outputs:
- factor_diag: float32 [512, 512], P(('row', 'col'))
- factor_panel: float32 [8192, 512], P('row', 'col')
- schur: float32 [8192, 8192], P('row', 'col')
The draws below stay inside these ranges and needn't reach their ends.
Inputs may be any that keep to these rules, and one draw needn't show every extreme that they name: diag_block is symmetric positive definite: a covariance matrix plus the identity. panel_block holds the covariances between slab points and panel points of the same covariance. trailing is symmetric, and together with diag_block and panel_block forms one positive definite covariance matrix plus the identity.
All inputs are finite; a program needn't handle non-finite values.
Results may differ from the reference program's by a relative error of at most 0.00028.
Values sent between devices are 32-bit elements; how exact they have to be, the bound alone decides.
A program may use at most 64 MiB of HBM per device.

```python
import math
import jax
import jax.numpy as jnp
from jax import lax

NB = 512
INPUTS = 12
SR = 8192


def scaled_points(key):
    base = jax.random.uniform(jax.random.fold_in(key, 101), (NB + SR, INPUTS), jnp.float32)
    lengths = jnp.exp(jax.random.uniform(jax.random.fold_in(key, 102), (INPUTS,), jnp.float32, math.log(0.3), math.log(1.0)))
    return base / lengths[None, :]


def matern_five(first, second):
    squared = jnp.zeros((first.shape[0], second.shape[0]), jnp.float32)
    for column in range(INPUTS):
        differ = first[:, column][:, None] - second[:, column][None, :]
        squared = squared + differ * differ
    scaled = math.sqrt(5.0) * jnp.sqrt(squared)
    return (1.0 + scaled + scaled * scaled / 3.0) * jnp.exp(-scaled)


def draw_diag_block(key, part):
    points = scaled_points(key)[:NB]
    return matern_five(points, points) + jnp.eye(NB, dtype=jnp.float32)


def draw_panel_block(key, part):
    points = scaled_points(key)
    return matern_five(points[NB:], points[:NB])


def draw_trailing(key, part):
    points = scaled_points(key)[NB:]
    return matern_five(points, points) + jnp.eye(SR, dtype=jnp.float32)


def setup_inputs(seed: int = 0) -> dict:
    key_list = jax.random.split(jax.random.key(seed), 4)
    return {
        "diag_block": draw_diag_block(jax.random.fold_in(key_list[3], 71), 0),
        "panel_block": draw_panel_block(jax.random.fold_in(key_list[3], 71), 0),
        "trailing": draw_trailing(jax.random.fold_in(key_list[3], 71), 0),
    }


def reference(diag_block, panel_block, trailing):
    factor = jnp.linalg.cholesky(diag_block)
    solved = jax.scipy.linalg.solve_triangular(factor, panel_block.T, lower=True).T
    update = jnp.dot(solved.astype(jnp.float32), solved.T.astype(jnp.float32), precision=lax.Precision.HIGHEST, preferred_element_type=jnp.float32)
    return (factor, solved, trailing - update)
```

```python
import functools

import jax
import jax.numpy as jnp
from jax import lax
from jax.experimental import pallas as pl
from jax.experimental.pallas import tpu as pltpu
from jax.sharding import PartitionSpec as P

NB = 512
F32 = jnp.float32
BF16 = jnp.bfloat16
MESH = pl.DeviceIdType.MESH
CHIPS = 16
COLS = 8


def gather_kernel(a_ref, b_ref, g_ref, br_ref, bc_ref, m_ref,
                  as_sem, ar_sem, rs_sem, rr_sem, ms_sem, mr_sem, ps_sem, pr_sem, loc_sem):
    row = lax.axis_index("row")
    z = lax.axis_index("col")
    chip = row // 2
    core = row % 2

    def at_z(k):
        return {"row": row, "col": (z + k) % COLS}

    def at_chip(k):
        return {"row": ((chip + k) % CHIPS) * 2 + core, "col": z}

    partner = {"row": row + 1 - 2 * core, "col": z}

    def copy(src, dst, ssem, rsem, device):
        return pltpu.make_async_remote_copy(
            src_ref=src, dst_ref=dst, send_sem=ssem, recv_sem=rsem,
            device_id=device, device_id_type=MESH)

    barrier = pltpu.get_barrier_semaphore()
    for k in range(1, COLS):
        pl.semaphore_signal(barrier, inc=1, device_id=at_z(k), device_id_type=MESH)
    for k in range(1, CHIPS):
        pl.semaphore_signal(barrier, inc=1, device_id=at_chip(k), device_id_type=MESH)
    pl.semaphore_signal(barrier, inc=1, device_id=partner, device_id_type=MESH)
    own_a = pltpu.make_async_copy(a_ref, g_ref.at[chip, core, z], loc_sem.at[0])
    own_b = pltpu.make_async_copy(b_ref, br_ref.at[z], loc_sem.at[1])
    own_a.start()
    own_b.start()
    pl.semaphore_wait(barrier, COLS + CHIPS - 1)

    a_z = [copy(a_ref, g_ref.at[chip, core, z], as_sem.at[k - 1], ar_sem.at[k - 1], at_z(k))
           for k in range(1, COLS)]
    for c in a_z:
        c.start()

    move1 = copy(b_ref, m_ref, ms_sem.at[0], mr_sem.at[0], at_chip(2 * z))
    move1_own = pltpu.make_async_copy(b_ref, m_ref, loc_sem.at[2])

    @pl.when(z != 0)
    def _():
        move1.start()

    @pl.when(z == 0)
    def _():
        move1_own.start()

    own_a.wait()
    for c in a_z:
        c.wait()
    mine = g_ref.at[chip, core]
    a_p = [copy(mine, mine, as_sem.at[6 + k], ar_sem.at[6 + k], at_chip(k))
           for k in range(1, CHIPS)]
    for c in a_p:
        c.start()

    @pl.when(z != 0)
    def _():
        move1.wait()

    @pl.when(z == 0)
    def _():
        move1_own.wait()

    src = (chip + CHIPS - 2 * z) % CHIPS
    plane = src // 2
    slot = bc_ref.at[src % 2, core, z]
    move2 = copy(m_ref, slot, ms_sem.at[1], mr_sem.at[1], {"row": row, "col": plane})
    move2_own = pltpu.make_async_copy(m_ref, slot, loc_sem.at[3])

    @pl.when(plane != z)
    def _():
        move2.start()

    @pl.when(plane == z)
    def _():
        move2_own.start()

    b_z = [copy(b_ref, br_ref.at[z], rs_sem.at[k - 1], rr_sem.at[k - 1], at_z(k))
           for k in range(1, COLS)]
    for c in b_z:
        c.start()

    for c in a_p:
        c.wait()
    half = g_ref.at[:, core]
    a_c = copy(half, half, as_sem.at[22], ar_sem.at[22], partner)
    a_c.start()

    @pl.when(plane != z)
    def _():
        move2.wait()

    @pl.when(plane == z)
    def _():
        move2_own.wait()

    held = bc_ref.at[chip % 2, core, (chip // 2 + COLS - z) % COLS]
    b_p = [copy(held, held, ps_sem.at[k - 1], pr_sem.at[k - 1], at_chip(k))
           for k in range(1, CHIPS)]
    for c in b_p:
        c.start()
    a_c.wait()
    for c in b_p:
        c.wait()
    bhalf = bc_ref.at[:, core]
    b_c = copy(bhalf, bhalf, ps_sem.at[15], pr_sem.at[15], partner)
    b_c.start()
    own_b.wait()
    for c in b_z:
        c.wait()
    b_c.wait()


def gather(a_tile, b_t):
    vmem = pl.BlockSpec(memory_space=pltpu.VMEM)
    dma = pltpu.SemaphoreType.DMA
    return pl.pallas_call(
        gather_kernel,
        out_shape=(
            jax.ShapeDtypeStruct((CHIPS, 2, COLS, 8, 128), F32),
            jax.ShapeDtypeStruct((COLS, 64, 256), F32),
            jax.ShapeDtypeStruct((2, 2, COLS, 64, 256), F32),
        ),
        in_specs=[vmem] * 2,
        out_specs=(vmem,) * 3,
        scratch_shapes=[
            pltpu.VMEM((64, 256), F32),
            dma((23,)), dma((23,)), dma((7,)), dma((7,)), dma((2,)), dma((2,)),
            dma((16,)), dma((16,)), dma((4,)),
        ],
        compiler_params=pltpu.CompilerParams(collective_id=0, has_side_effects=True),
        name="gather",
    )(a_tile, b_t)


def split(x):
    high = x.astype(BF16)
    return high, (x - high.astype(F32)).astype(BF16)


def mm(a, b, dims):
    return lax.dot_general(a, b, (dims, ((), ())), preferred_element_type=F32)


NN = ((1,), (0,))
NT = ((1,), (1,))


def dot3s(a, b, dims=NN):
    return mm(a[0], b[0], dims) + (mm(a[0], b[1], dims) + mm(a[1], b[0], dims))


def dot3(a, b, dims=NN):
    return dot3s(split(a), split(b), dims)


def scales(top, tol):
    e = (top - 1.0) / (top + 1.0)
    out = []
    while e > tol:
        m = 2.0 / (2.0 - e * e)
        out.append(m)
        e = e * e * m / 2.0
    return 2.0 / (1.0 + top), out


def eye(n):
    return (lax.broadcasted_iota(jnp.int32, (n, n), 0)
            == lax.broadcasted_iota(jnp.int32, (n, n), 1)).astype(F32)


TOL = 3e-3


def inverse(mats, top, one):
    start, steps = scales(top, TOL)
    n = one.shape[0]
    xs = [None] * len(mats)
    rs = [start * m for m in mats]
    for k, m in enumerate(steps):
        last = k == len(steps) - 1
        ns = [(2.0 * m) * one - m * r for r in rs]
        if k == 0:
            xs = [start * nn for nn in ns]
            if not last:
                rs = [dot3(r, nn) for r, nn in zip(rs, ns)]
        elif last:
            xs = [dot3(x, nn) for x, nn in zip(xs, ns)]
        else:
            both = [dot3(jnp.concatenate([x, r], 0), nn) for x, r, nn in zip(xs, rs, ns)]
            xs = [t[:n] for t in both]
            rs = [t[n:] for t in both]
    return xs


def tri_low(n):
    i = lax.broadcasted_iota(jnp.int32, (n, n), 0)
    j = lax.broadcasted_iota(jnp.int32, (n, n), 1)
    return i, j


def factor_kernel(g_ref, br_ref, bc_ref, t_ref, fd_ref, fp_ref, s_ref, a4_ref, a_ref, w_ref, l_ref):
    row = lax.axis_index("row")
    z = lax.axis_index("col")
    for s in range(2):
        for l in range(4):
            a4_ref[l, pl.ds(s, 256, stride=2), :] = (
                g_ref[pl.ds(2 * l + s, 256, stride=8), :])
    for l in range(4):
        a_ref[:, l * 128:(l + 1) * 128] = a4_ref[l]
    one256 = eye(256)
    one128 = eye(128)
    a11 = a_ref[0:256, 0:256]
    a21 = a_ref[256:512, 0:256]
    x = inverse([a11], 257.0, one256)[0]
    g1 = dot3(a21, x)
    blocks = [a11, a_ref[256:512, 256:512] - dot3(g1, a21, NT)]
    xs = inverse([m[:128, :128] for m in blocks], 129.0, one128)
    tiles = []
    g2 = []
    for m, x in zip(blocks, xs):
        low = m[128:, :128]
        g = dot3(low, x)
        g2.append(g)
        tiles += [m[:128, :128], m[128:, 128:] - dot3(g, low, NT)]
    g1p = jnp.concatenate([g1[:128], g1[128:] - dot3(g2[1], g1[:128])], 0)
    i, j = tri_low(128)
    ts = None
    b = 64
    while b >= 1:
        bi, bj = i // b, j // b
        same = bi == bj
        even = bi % 2 == 0
        m21 = jnp.logical_and(bi == bj + 1, bj % 2 == 0)
        lows = [jnp.where(m21, m, 0.0) for m in tiles]
        odd_one = jnp.where(even, 0.0, one128)
        keep = jnp.logical_and(same, even)
        ds = [jnp.where(keep, m, 0.0) + odd_one for m in tiles]
        if b > 1:
            xs = inverse(ds, 1.0 + b, one128)
        else:
            xs = [jnp.where(keep, 1.0 / d, 0.0) + odd_one for d in
                  [jnp.where(i == j, dd, 1.0) for dd in ds]]
        gs = [dot3(lo, x) for lo, x in zip(lows, xs)]
        tiles = [jnp.where(same, m, 0.0) - dot3(g, lo, NT) for m, g, lo in zip(tiles, gs, lows)]
        if ts is None:
            ts = [one128 - g for g in gs]
        else:
            ts = [t - dot3(g, t) for t, g in zip(ts, gs)]
        b //= 2
    ts = [lax.rsqrt(jnp.sum(jnp.where(i == j, m, 0.0), axis=1, keepdims=True)) * t
          for m, t in zip(tiles, ts)]
    zero = jnp.zeros((128, 128), F32)
    hs = []
    for k in range(2):
        hs.append(jnp.concatenate([
            jnp.concatenate([ts[2 * k], zero], 1),
            jnp.concatenate([-dot3(ts[2 * k + 1], g2[k]), ts[2 * k + 1]], 1)], 0))
    w11, w22 = hs
    w21 = -jnp.concatenate([dot3(ts[2], g1p[:128]), dot3(ts[3], g1p[128:])], 0)
    i, j = tri_low(256)
    low_half = jnp.where(i > j, 1.0, jnp.where(i == j, 0.5, 0.0))
    a_s = split(a_ref[...])

    def cut(p, r, c):
        return p[0][r, c], p[1][r, c]
    lo, hi, al = slice(0, 256), slice(256, 512), slice(0, 512)
    for _ in range(2):
        w1s = split(w11)
        w2s = split(jnp.concatenate([w21, w22], 1))
        wa1 = split(dot3s(w1s, cut(a_s, lo, lo)))
        wa2 = split(dot3s(w2s, a_s))
        e11 = (dot3s(wa1, w1s, NT) - one256) * low_half
        e21 = dot3s(cut(wa2, al, lo), w1s, NT)
        e22 = (dot3s(wa2, w2s, NT) - one256) * low_half
        p11, p21, p22 = e11.astype(BF16), e21.astype(BF16), e22.astype(BF16)
        w11 = w11 - mm(p11, w1s[0], NN)
        nw2 = mm(p22, w2s[0], NN)
        w21 = w21 - nw2[:, :256] - mm(p21, w1s[0], NN)
        w22 = w22 - nw2[:, 256:]
    w_ref[0:256, 0:256] = w11
    w_ref[0:256, 256:512] = jnp.zeros((256, 256), F32)
    w_ref[256:512, 0:256] = w21
    w_ref[256:512, 256:512] = w22

    w_s = split(w_ref[...])
    d = row * COLS + z
    base = d // 4
    l_ref[...] = dot3s(split(a_ref[pl.ds(pl.multiple_of(base * 8, 8), 8), :]), w_s, NT)
    lane = lax.broadcasted_iota(jnp.int32, (1, 512), 1)
    for s in range(2):
        line = l_ref[pl.ds(2 * (d % 4) + s, 1), :]
        line = jnp.where(lane <= 2 * d + s, line, 0.0)
        for l in range(4):
            fd_ref[2 * l + s:2 * l + s + 1, :] = line[:, l * 128:(l + 1) * 128]

    b_t = br_ref[...]
    fp_ref[...] = dot3(w_ref[pl.ds(pl.multiple_of(z * 64, 64), 64), :], b_t)
    p_r = dot3s(split(b_t.T), w_s, NT)
    u_s = split(dot3s(split(p_r), w_s))
    for q in range(4):
        cols = slice(q * 256, (q + 1) * 256)
        s_ref[:, cols] = t_ref[:, cols] - dot3s(u_s, split(bc_ref[q]))


def factor(g, br, bc, trailing):
    vmem = pl.BlockSpec(memory_space=pltpu.VMEM)
    return pl.pallas_call(
        factor_kernel,
        out_shape=(
            jax.ShapeDtypeStruct((8, 128), F32),
            jax.ShapeDtypeStruct((64, 256), F32),
            jax.ShapeDtypeStruct((256, 1024), F32),
        ),
        in_specs=[vmem] * 4,
        out_specs=(vmem,) * 3,
        scratch_shapes=[
            pltpu.VMEM((4, 512, 128), F32),
            pltpu.VMEM((512, 512), F32),
            pltpu.VMEM((512, 512), F32),
            pltpu.VMEM((8, 512), F32),
        ],
        compiler_params=pltpu.CompilerParams(vmem_limit_bytes=60 * 1024 * 1024),
        name="factor",
    )(g, br, bc, trailing)


def per_device(diag_block, panel_block, trailing):
    tile = diag_block.reshape(2, 4, 128).transpose(1, 0, 2).reshape(8, 128)
    g, br, bc = gather(tile, panel_block.T)
    fd, fp, schur = factor(
        g.reshape(2048, 128), br.reshape(512, 256), bc.reshape(4, 512, 256), trailing)
    fd = fd.reshape(4, 2, 128).transpose(1, 0, 2).reshape(2, 512)
    return fd, fp.T, schur


def solution(mesh):
    return jax.shard_map(
        per_device,
        mesh=mesh,
        in_specs=(P(("row", "col"), None), P("row", "col"), P("row", "col")),
        out_specs=(P(("row", "col"), None), P("row", "col"), P("row", "col")),
        check_vma=False,
    )
```

```python
import functools

import jax
import jax.numpy as jnp
from jax import lax
from jax.experimental import pallas as pl
from jax.experimental.pallas import tpu as pltpu
from jax.sharding import PartitionSpec as P

NB = 512
F32 = jnp.float32
BF16 = jnp.bfloat16
MESH = pl.DeviceIdType.MESH
CHIPS = 16
COLS = 8


def split(x):
    high = x.astype(BF16)
    return high, (x - high.astype(F32)).astype(BF16)


def mm(a, b, dims):
    return lax.dot_general(a, b, (dims, ((), ())), preferred_element_type=F32)


NN = ((1,), (0,))
NT = ((1,), (1,))


def dot3s(a, b, dims=NN):
    return mm(a[0], b[0], dims) + (mm(a[0], b[1], dims) + mm(a[1], b[0], dims))


def dot3(a, b, dims=NN):
    return dot3s(split(a), split(b), dims)


def dotp(a, b):
    bh, bl = split(b)
    w = jnp.concatenate([bh, bl], 1)
    out = mm(jnp.concatenate(split(a), 1), jnp.concatenate([w, w], 0), NN)
    n = b.shape[1]
    return out[:, :n] + out[:, n:]


def dotp_t(a, b):
    bh, bl = split(b)
    w = jnp.concatenate([jnp.concatenate([bh, bh], 1), jnp.concatenate([bl, bl], 1)], 0)
    out = mm(jnp.concatenate(split(a), 1), w, NT)
    n = b.shape[0]
    return out[:, :n] + out[:, n:]


def scales(top, tol):
    e = (top - 1.0) / (top + 1.0)
    out = []
    while e > tol:
        m = 2.0 / (2.0 - e * e)
        out.append(m)
        e = e * e * m / 2.0
    return 2.0 / (1.0 + top), out


def grid2(n):
    i = lax.broadcasted_iota(jnp.int32, (n, n), 0)
    j = lax.broadcasted_iota(jnp.int32, (n, n), 1)
    return i, j


TOL = {256: 3e-4, 128: 1e-3, 64: 1e-3, 32: 1e-3, 16: 1e-3}
BASE = 16


def half_split(m, n, dot, dot_t):
    i, j = grid2(n)
    start, steps = scales(1.0 + n, TOL[n])
    zs = [start * x[:, :n] for x in m]
    for k, s in enumerate(steps):
        ns = [jnp.where(i == j, 2.0 * s, 0.0) - s * z[:n] for z in zs]
        if k == len(steps) - 1:
            zs = [z[n:] for z in zs]
        zs = [dot(z, nn) for z, nn in zip(zs, ns)]
    return zs, [x[n:, n:] - dot_t(z, x[n:, :n]) for x, z in zip(m, zs)]


def base_factors(tiles):
    sub = lax.broadcasted_iota(jnp.int32, (BASE, 128), 0)
    lane = lax.broadcasted_iota(jnp.int32, (BASE, 128), 1)
    groups = 128 // BASE
    rows = []
    for m in tiles:
        acc = None
        for g in range(groups):
            part = jnp.where(lane // BASE == g, m[g * BASE:(g + 1) * BASE], 0.0)
            acc = part if acc is None else acc + part
        rows.append(acc)
    ident = jnp.where(sub == lane % BASE, 1.0, 0.0)
    es = [ident] * len(tiles)
    for p in range(BASE):
        index = (lane // BASE) * BASE + p
        for t in range(len(tiles)):
            col = jnp.take_along_axis(rows[t], index, axis=1, mode="promise_in_bounds")
            root = lax.rsqrt(col[p:p + 1])
            e_row = es[t][p:p + 1] * root
            if p < BASE - 1:
                a_row = rows[t][p:p + 1] * (root * root)
                below = jnp.where(sub > p, col, 0.0)
                rows[t] = rows[t] - below * a_row
                es[t] = jnp.where(sub == p, e_row, es[t] - below * (e_row * root))
            else:
                es[t] = jnp.where(sub == p, e_row, es[t])
    return [jnp.concatenate([jnp.where(lane // BASE == g, e, 0.0) for g in range(groups)], 0)
            for e in es]


def factor_inverse(a, between=lambda: None):
    (g1,), (s,) = half_split([a[...]], 256, dot3, lambda x, y: dot3(x, y, NT))
    blocks = [a[0:256, 0:256], s]
    g2, s2 = half_split(blocks, 128, dotp, dotp_t)
    tiles = [blocks[0][:128, :128], s2[0], blocks[1][:128, :128], s2[1]]
    i, j = grid2(128)
    ts = None
    b = 64
    while b >= BASE:
        bi, bj = i // b, j // b
        start, steps = scales(1.0 + b, TOL[b])
        pair = jnp.logical_and(i // (2 * b) == j // (2 * b), bj % 2 == 0)
        even = bi % 2 == 0
        low = jnp.logical_and(pair, jnp.logical_not(even))
        diag = jnp.logical_and(i == j, even)
        lows = [jnp.where(low, m, 0.0) for m in tiles]
        zs = [jnp.where(pair, start * m, 0.0) for m in tiles]
        for sc in steps:
            ns = [jnp.where(diag, 2.0 * sc, 0.0) - jnp.where(even, sc * z, 0.0) for z in zs]
            zs = [dotp(z, nn) for z, nn in zip(zs, ns)]
        gs = [jnp.where(even, 0.0, z) for z in zs]
        tiles = [jnp.where(bi == bj, m, 0.0) - dotp_t(g, lo) for m, g, lo in zip(tiles, gs, lows)]
        if ts is None:
            ts = [jnp.where(i == j, 1.0, 0.0) - g for g in gs]
        else:
            ts = [t - dotp(g, t) for t, g in zip(ts, gs)]
        b //= 2
    g1p = jnp.concatenate([g1[:128], g1[128:] - dotp(g2[1], g1[:128])], 0)
    bases = base_factors(tiles)
    between()
    ts = [dotp(e, t) for e, t in zip(bases, ts)]
    zero = jnp.zeros((128, 128), F32)
    w11, w22 = [jnp.concatenate([
        jnp.concatenate([ts[2 * k], zero], 1),
        jnp.concatenate([-dotp(ts[2 * k + 1], g2[k]), ts[2 * k + 1]], 1)], 0) for k in range(2)]
    w21 = -jnp.concatenate([dotp(ts[2], g1p[:128]), dotp(ts[3], g1p[128:])], 0)

    i, j = grid2(256)
    one = jnp.where(i == j, 1.0, 0.0)
    low_half = jnp.where(i > j, 1.0, jnp.where(i == j, 0.5, 0.0))
    a_s = split(a[...])
    w1s = split(w11)
    w2s = split(jnp.concatenate([w21, w22], 1))
    wa1 = split(dot3s(w1s, [x[:256, :256] for x in a_s]))
    wa2 = split(dot3s(w2s, a_s))
    p11 = ((dot3s(wa1, w1s, NT) - one) * low_half).astype(BF16)
    p21 = dot3s([x[:, :256] for x in wa2], w1s, NT).astype(BF16)
    p22 = ((dot3s(wa2, w2s, NT) - one) * low_half).astype(BF16)
    n11 = w11 - mm(p11, w1s[0], NN)
    nw2 = mm(p22, w2s[0], NN)
    return n11, w21 - nw2[:, :256] - mm(p21, w1s[0], NN), w22 - nw2[:, 256:]


def step_kernel(d_ref, b_ref, bc_ref, fd_ref, fp_ref, uh_ref, ul_ref,
                g_ref, br_ref, m_ref, a4_ref, a_ref, w_ref, l_ref, bt_ref,
                as_sem, ar_sem, rs_sem, rr_sem, ms_sem, mr_sem, ps_sem, pr_sem, loc_sem):
    row = lax.axis_index("row")
    z = lax.axis_index("col")
    chip = row // 2
    core = row % 2

    def at_z(k):
        return {"row": row, "col": (z + k) % COLS}

    def at_chip(k):
        return {"row": ((chip + k) % CHIPS) * 2 + core, "col": z}

    partner = {"row": row + 1 - 2 * core, "col": z}

    def copy(src, dst, ssem, rsem, device):
        return pltpu.make_async_remote_copy(
            src_ref=src, dst_ref=dst, send_sem=ssem, recv_sem=rsem,
            device_id=device, device_id_type=MESH)

    barrier = pltpu.get_barrier_semaphore()
    for k in range(1, COLS):
        pl.semaphore_signal(barrier, inc=1, device_id=at_z(k), device_id_type=MESH)
    for k in range(1, CHIPS):
        pl.semaphore_signal(barrier, inc=1, device_id=at_chip(k), device_id_type=MESH)
    pl.semaphore_signal(barrier, inc=1, device_id=partner, device_id_type=MESH)
    def tile(c, k, zz):
        first = pl.multiple_of(((c * 2 + k) * COLS + zz) * 8, 8)
        return g_ref.at[pl.ds(first, 8)]

    own_a = pltpu.make_async_copy(d_ref, tile(chip, core, z), loc_sem.at[0])
    own_b = pltpu.make_async_copy(b_ref, br_ref.at[z], loc_sem.at[1])
    own_a.start()
    own_b.start()
    pl.semaphore_wait(barrier, COLS + CHIPS - 1)

    a_z = [copy(d_ref, tile(chip, core, z), as_sem.at[k - 1], ar_sem.at[k - 1], at_z(k))
           for k in range(1, COLS)]
    for c in a_z:
        c.start()

    move1 = copy(b_ref, m_ref, ms_sem.at[0], mr_sem.at[0], at_chip(2 * z))
    move1_own = pltpu.make_async_copy(b_ref, m_ref, loc_sem.at[2])

    @pl.when(z != 0)
    def _():
        move1.start()

    @pl.when(z == 0)
    def _():
        move1_own.start()

    own_a.wait()
    for c in a_z:
        c.wait()

    def line(c):
        return g_ref.at[pl.ds(pl.multiple_of((c * 2 + core) * COLS * 8, 64), 64)]

    a_p = [copy(line(chip), line(chip), as_sem.at[6 + k], ar_sem.at[6 + k], at_chip(k))
           for k in range(1, CHIPS)]
    for c in a_p:
        c.start()

    @pl.when(z != 0)
    def _():
        move1.wait()

    @pl.when(z == 0)
    def _():
        move1_own.wait()

    src = (chip + CHIPS - 2 * z) % CHIPS
    plane = src // 2
    slot = bc_ref.at[src % 2, core, z]
    move2 = copy(m_ref, slot, ms_sem.at[1], mr_sem.at[1], {"row": row, "col": plane})
    move2_own = pltpu.make_async_copy(m_ref, slot, loc_sem.at[3])

    @pl.when(plane != z)
    def _():
        move2.start()

    @pl.when(plane == z)
    def _():
        move2_own.start()

    b_z = [copy(b_ref, br_ref.at[z], rs_sem.at[k - 1], rr_sem.at[k - 1], at_z(k))
           for k in range(1, COLS)]
    for c in b_z:
        c.start()

    a_c = []
    for k in range(CHIPS):
        c = (chip + CHIPS - k) % CHIPS
        if k:
            a_p[k - 1].wait_recv()
        a_c.append(copy(line(c), line(c), as_sem.at[22 + k], ar_sem.at[22 + k], partner))
        a_c[-1].start()
    for c in a_p:
        c.wait_send()

    @pl.when(plane != z)
    def _():
        move2.wait()

    @pl.when(plane == z)
    def _():
        move2_own.wait()

    held = bc_ref.at[chip % 2, core, (chip // 2 + COLS - z) % COLS]
    b_p = [copy(held, held, ps_sem.at[k - 1], pr_sem.at[k - 1], at_chip(k))
           for k in range(1, CHIPS)]
    for c in b_p:
        c.start()
    for c in a_c:
        c.wait()

    for s in range(2):
        for l in range(4):
            a4_ref[l, pl.ds(s, 256, stride=2), :] = (
                g_ref[pl.ds(2 * l + s, 256, stride=8), :])
    for l in range(4):
        a_ref[:, l * 128:(l + 1) * 128] = a4_ref[l]

    bhalf = bc_ref.at[:, core]
    b_c = copy(bhalf, bhalf, ps_sem.at[15], pr_sem.at[15], partner)

    def between():
        own_b.wait()
        for c in b_z:
            c.wait()
        bt_ref[...] = br_ref[...].reshape(512, 256).T
        for c in b_p:
            c.wait()
        b_c.start()

    w11, w21, w22 = factor_inverse(a_ref, between)
    w_ref[0:256, 0:256] = w11
    w_ref[0:256, 256:512] = jnp.zeros((256, 256), F32)
    w_ref[256:512, 0:256] = w21
    w_ref[256:512, 256:512] = w22

    w1s = split(w11)
    w2s = split(jnp.concatenate([w21, w22], 1))
    d = row * COLS + z
    mine = split(a_ref[pl.ds(pl.multiple_of((d // 4) * 8, 8), 8), :])
    l_ref[:, 0:256] = dot3s([x[:, :256] for x in mine], w1s, NT)
    l_ref[:, 256:512] = dot3s(mine, w2s, NT)
    lane = lax.broadcasted_iota(jnp.int32, (1, 512), 1)
    for s in range(2):
        line_s = l_ref[pl.ds(2 * (d % 4) + s, 1), :]
        line_s = jnp.where(lane <= 2 * d + s, line_s, 0.0)
        for l in range(4):
            fd_ref[2 * l + s:2 * l + s + 1, :] = line_s[:, l * 128:(l + 1) * 128]

    fp_ref[...] = dot3(w_ref[pl.ds(pl.multiple_of(z * 64, 64), 64), :],
                       br_ref[...].reshape(512, 256))
    b_s = split(bt_ref[...])
    p1 = split(dot3s([x[:, :256] for x in b_s], w1s, NT))
    p2 = split(dot3s(b_s, w2s, NT))
    u2 = dot3s(p2, w2s)
    u1 = u2[:, :256] + dot3s(p1, w1s)
    for cols, u in ((slice(0, 256), u1), (slice(256, 512), u2[:, 256:])):
        uh_ref[:, cols], ul_ref[:, cols] = split(u)
    b_c.wait()


def step(d_tile, b_t):
    vmem = pl.BlockSpec(memory_space=pltpu.VMEM)
    dma = pltpu.SemaphoreType.DMA
    return pl.pallas_call(
        step_kernel,
        out_shape=(
            jax.ShapeDtypeStruct((2, 2, COLS, 64, 256), F32),
            jax.ShapeDtypeStruct((8, 128), F32),
            jax.ShapeDtypeStruct((64, 256), F32),
            jax.ShapeDtypeStruct((256, 512), BF16),
            jax.ShapeDtypeStruct((256, 512), BF16),
        ),
        in_specs=[vmem] * 2,
        out_specs=(pl.BlockSpec(memory_space=pl.ANY),) + (vmem,) * 4,
        scratch_shapes=[
            pltpu.VMEM((2048, 128), F32),
            pltpu.VMEM((COLS, 64, 256), F32),
            pltpu.VMEM((64, 256), F32),
            pltpu.VMEM((4, 512, 128), F32),
            pltpu.VMEM((512, 512), F32),
            pltpu.VMEM((512, 512), F32),
            pltpu.VMEM((8, 512), F32),
            pltpu.VMEM((256, 512), F32),
            dma((38,)), dma((38,)), dma((7,)), dma((7,)), dma((2,)), dma((2,)),
            dma((16,)), dma((16,)), dma((4,)),
        ],
        compiler_params=pltpu.CompilerParams(
            collective_id=0, has_side_effects=True, vmem_limit_bytes=40 * 1024 * 1024),
        name="step",
    )(d_tile, b_t)


def update_kernel(uh_ref, ul_ref, bc_ref, t_ref, fd_in, fp_in, s_ref, fd_ref, fp_ref):
    s_ref[...] = t_ref[...] - dot3s((uh_ref[...], ul_ref[...]), split(bc_ref[...]))

    @pl.when(pl.program_id(0) == 0)
    def _():
        fd_ref[...] = fd_in[...]
        fp_ref[...] = fp_in[...]


def update(uh, ul, bc, trailing, fd, fp):
    whole = lambda shape: pl.BlockSpec(shape, lambda q: (0, 0))
    block = pl.BlockSpec((256, 256), lambda q: (0, q))
    return pl.pallas_call(
        update_kernel,
        grid=(4,),
        out_shape=(
            jax.ShapeDtypeStruct((256, 1024), F32),
            jax.ShapeDtypeStruct((8, 128), F32),
            jax.ShapeDtypeStruct((64, 256), F32),
        ),
        in_specs=[whole((256, 512)), whole((256, 512)),
                  pl.BlockSpec((None, 512, 256), lambda q: (q, 0, 0)), block,
                  whole((8, 128)), whole((64, 256))],
        out_specs=(block, whole((8, 128)), whole((64, 256))),
        compiler_params=pltpu.CompilerParams(vmem_limit_bytes=16 * 1024 * 1024),
        name="update",
    )(uh, ul, bc, trailing, fd, fp)


def per_device(diag_block, panel_block, trailing):
    tile = diag_block.reshape(2, 4, 128).transpose(1, 0, 2).reshape(8, 128)
    bc, fd, fp, uh, ul = step(tile, panel_block.T)
    schur, fd, fp = update(uh, ul, bc.reshape(4, 512, 256), trailing, fd, fp)
    fd = fd.reshape(4, 2, 128).transpose(1, 0, 2).reshape(2, 512)
    return fd, fp.T, schur


def solution(mesh):
    return jax.shard_map(
        per_device,
        mesh=mesh,
        in_specs=(P(("row", "col"), None), P("row", "col"), P("row", "col")),
        out_specs=(P(("row", "col"), None), P("row", "col"), P("row", "col")),
        check_vma=False,
    )
```

```python
import functools

import jax
import jax.numpy as jnp
from jax import lax
from jax.experimental import pallas as pl
from jax.experimental.pallas import tpu as pltpu
from jax.sharding import PartitionSpec as P

NB = 512
F32 = jnp.float32
BF16 = jnp.bfloat16
MESH = pl.DeviceIdType.MESH
CHIPS = 16
COLS = 8


def split(x):
    high = x.astype(BF16)
    return high, (x - high.astype(F32)).astype(BF16)


def mm(a, b, dims):
    return lax.dot_general(a, b, (dims, ((), ())), preferred_element_type=F32)


NN = ((1,), (0,))
NT = ((1,), (1,))


def dot3s(a, b, dims=NN):
    return mm(a[0], b[0], dims) + (mm(a[0], b[1], dims) + mm(a[1], b[0], dims))


def dot3(a, b, dims=NN):
    return dot3s(split(a), split(b), dims)


def dotp(a, b):
    bh, bl = split(b)
    w = jnp.concatenate([bh, bl], 1)
    out = mm(jnp.concatenate(split(a), 1), jnp.concatenate([w, w], 0), NN)
    n = b.shape[1]
    return out[:, :n] + out[:, n:]


def dotp_t(a, b):
    bh, bl = split(b)
    w = jnp.concatenate([jnp.concatenate([bh, bh], 1), jnp.concatenate([bl, bl], 1)], 0)
    out = mm(jnp.concatenate(split(a), 1), w, NT)
    n = b.shape[0]
    return out[:, :n] + out[:, n:]


def scales(top, tol):
    e = (top - 1.0) / (top + 1.0)
    out = []
    while e > tol:
        m = 2.0 / (2.0 - e * e)
        out.append(m)
        e = e * e * m / 2.0
    return 2.0 / (1.0 + top), out


def grid2(n):
    i = lax.broadcasted_iota(jnp.int32, (n, n), 0)
    j = lax.broadcasted_iota(jnp.int32, (n, n), 1)
    return i, j


TOL = {256: 3e-4, 128: 1e-3, 64: 1e-3, 32: 1e-3, 16: 1e-3}
BASE = 16


def half_split(m, n, dot, dot_t):
    i, j = grid2(n)
    start, steps = scales(1.0 + n, TOL[n])
    zs = [start * x[:, :n] for x in m]
    for k, s in enumerate(steps):
        ns = [jnp.where(i == j, 2.0 * s, 0.0) - s * z[:n] for z in zs]
        if k == len(steps) - 1:
            zs = [z[n:] for z in zs]
        zs = [dot(z, nn) for z, nn in zip(zs, ns)]
    return zs, [x[n:, n:] - dot_t(z, x[n:, :n]) for x, z in zip(m, zs)]


def base_factors(tiles):
    sub = lax.broadcasted_iota(jnp.int32, (BASE, 128), 0)
    lane = lax.broadcasted_iota(jnp.int32, (BASE, 128), 1)
    groups = 128 // BASE
    rows = []
    for m in tiles:
        acc = None
        for g in range(groups):
            part = jnp.where(lane // BASE == g, m[g * BASE:(g + 1) * BASE], 0.0)
            acc = part if acc is None else acc + part
        rows.append(acc)
    ident = jnp.where(sub == lane % BASE, 1.0, 0.0)
    es = [ident] * len(tiles)
    for p in range(BASE):
        index = (lane // BASE) * BASE + p
        for t in range(len(tiles)):
            col = jnp.take_along_axis(rows[t], index, axis=1, mode="promise_in_bounds")
            root = lax.rsqrt(col[p:p + 1])
            e_row = es[t][p:p + 1] * root
            if p < BASE - 1:
                a_row = rows[t][p:p + 1] * (root * root)
                below = jnp.where(sub > p, col, 0.0)
                rows[t] = rows[t] - below * a_row
                es[t] = jnp.where(sub == p, e_row, es[t] - below * (e_row * root))
            else:
                es[t] = jnp.where(sub == p, e_row, es[t])
    return [jnp.concatenate([jnp.where(lane // BASE == g, e, 0.0) for g in range(groups)], 0)
            for e in es]


def factor_inverse(a, between=lambda: None):
    (g1,), (s,) = half_split([a[...]], 256, dot3, lambda x, y: dot3(x, y, NT))
    blocks = [a[0:256, 0:256], s]
    g2, s2 = half_split(blocks, 128, dotp, dotp_t)
    tiles = [blocks[0][:128, :128], s2[0], blocks[1][:128, :128], s2[1]]
    i, j = grid2(128)
    ts = None
    b = 64
    while b >= BASE:
        bi, bj = i // b, j // b
        start, steps = scales(1.0 + b, TOL[b])
        pair = jnp.logical_and(i // (2 * b) == j // (2 * b), bj % 2 == 0)
        even = bi % 2 == 0
        low = jnp.logical_and(pair, jnp.logical_not(even))
        diag = jnp.logical_and(i == j, even)
        lows = [jnp.where(low, m, 0.0) for m in tiles]
        zs = [jnp.where(pair, start * m, 0.0) for m in tiles]
        for sc in steps:
            ns = [jnp.where(diag, 2.0 * sc, 0.0) - jnp.where(even, sc * z, 0.0) for z in zs]
            zs = [dotp(z, nn) for z, nn in zip(zs, ns)]
        gs = [jnp.where(even, 0.0, z) for z in zs]
        tiles = [jnp.where(bi == bj, m, 0.0) - dotp_t(g, lo) for m, g, lo in zip(tiles, gs, lows)]
        if ts is None:
            ts = [jnp.where(i == j, 1.0, 0.0) - g for g in gs]
        else:
            ts = [t - dotp(g, t) for t, g in zip(ts, gs)]
        b //= 2
    g1p = jnp.concatenate([g1[:128], g1[128:] - dotp(g2[1], g1[:128])], 0)
    bases = base_factors(tiles)
    between()
    ts = [dotp(e, t) for e, t in zip(bases, ts)]
    zero = jnp.zeros((128, 128), F32)
    w11, w22 = [jnp.concatenate([
        jnp.concatenate([ts[2 * k], zero], 1),
        jnp.concatenate([-dotp(ts[2 * k + 1], g2[k]), ts[2 * k + 1]], 1)], 0) for k in range(2)]
    w21 = -jnp.concatenate([dotp(ts[2], g1p[:128]), dotp(ts[3], g1p[128:])], 0)

    i, j = grid2(256)
    one = jnp.where(i == j, 1.0, 0.0)
    low_half = jnp.where(i > j, 1.0, jnp.where(i == j, 0.5, 0.0))
    a_s = split(a[...])
    w1s = split(w11)
    w2s = split(jnp.concatenate([w21, w22], 1))
    wa1 = split(dot3s(w1s, [x[:256, :256] for x in a_s]))
    wa2 = split(dot3s(w2s, a_s))
    p11 = ((dot3s(wa1, w1s, NT) - one) * low_half).astype(BF16)
    p21 = dot3s([x[:, :256] for x in wa2], w1s, NT).astype(BF16)
    p22 = ((dot3s(wa2, w2s, NT) - one) * low_half).astype(BF16)
    n11 = w11 - mm(p11, w1s[0], NN)
    nw2 = mm(p22, w2s[0], NN)
    return n11, w21 - nw2[:, :256] - mm(p21, w1s[0], NN), w22 - nw2[:, 256:]


def step_kernel(d_ref, b_ref, t_ref, bc_ref, fd_ref, fp_ref, uh_ref, ul_ref, to_ref,
                g_ref, br_ref, m_ref, a4_ref, a_ref, w_ref, l_ref, bt_ref,
                az_s, az_r, ax_s, ax_r, ay_s, ay_r, ac_s, ac_r,
                bz_s, bz_r, mv_s, mv_r, bx_s, bx_r, by_s, by_r, bk_s, bk_r, loc_sem):
    row = lax.axis_index("row")
    z = lax.axis_index("col")
    chip = row // 2
    core = row % 2
    y = chip // 4
    x = chip % 4

    def at_z(k):
        return {"row": row, "col": (z + k) % COLS}

    def at_chip(k):
        return {"row": ((chip + k) % CHIPS) * 2 + core, "col": z}

    def at_x(k):
        return {"row": (y * 4 + (x + k) % 4) * 2 + core, "col": z}

    def at_y(k):
        return {"row": (((y + k) % 4) * 4 + x) * 2 + core, "col": z}

    partner = {"row": row + 1 - 2 * core, "col": z}

    def copy(src, dst, ssem, rsem, device):
        return pltpu.make_async_remote_copy(
            src_ref=src, dst_ref=dst, send_sem=ssem, recv_sem=rsem,
            device_id=device, device_id_type=MESH)

    def fan(ref, ssem, rsem, first, where, n):
        return [copy(ref, ref, ssem.at[first + k - 1], rsem.at[first + k - 1], where(k))
                for k in range(1, n + 1)]

    barrier = pltpu.get_barrier_semaphore()
    for k in range(1, COLS):
        pl.semaphore_signal(barrier, inc=1, device_id=at_z(k), device_id_type=MESH)
    for k in range(1, CHIPS):
        pl.semaphore_signal(barrier, inc=1, device_id=at_chip(k), device_id_type=MESH)
    pl.semaphore_signal(barrier, inc=1, device_id=partner, device_id_type=MESH)
    own_tile = g_ref.at[y, x, core, z]
    own_a = pltpu.make_async_copy(d_ref, own_tile, loc_sem.at[0])
    own_b = pltpu.make_async_copy(b_ref, br_ref.at[z], loc_sem.at[1])
    own_t = pltpu.make_async_copy(t_ref, to_ref, loc_sem.at[4])
    own_a.start()
    own_b.start()
    pl.semaphore_wait(barrier, COLS + CHIPS - 1)

    a_z = [copy(d_ref, own_tile, az_s.at[k - 1], az_r.at[k - 1], at_z(k))
           for k in range(1, COLS)]
    for c in a_z:
        c.start()

    move1 = copy(b_ref, m_ref, mv_s.at[0], mv_r.at[0], at_chip(2 * z))
    move1_own = pltpu.make_async_copy(b_ref, m_ref, loc_sem.at[2])

    @pl.when(z != 0)
    def _():
        move1.start()

    @pl.when(z == 0)
    def _():
        move1_own.start()

    own_t.start()
    own_a.wait()
    for c in a_z:
        c.wait()

    lo, hi = pl.ds(0, 4), pl.ds(4, 4)
    a_x = fan(g_ref.at[y, x, core, lo], ax_s, ax_r, 0, at_x, 3)
    a_y = fan(g_ref.at[y, x, core, hi], ay_s, ay_r, 0, at_y, 3)
    for p, q in zip(a_x, a_y):
        p.start()
        q.start()

    @pl.when(z != 0)
    def _():
        move1.wait()

    @pl.when(z == 0)
    def _():
        move1_own.wait()

    src = (chip + CHIPS - 2 * z) % CHIPS
    plane = src // 2
    slot = bc_ref.at[core, y, x]
    move2 = copy(m_ref, slot, mv_s.at[1], mv_r.at[1], {"row": row, "col": plane})
    move2_own = pltpu.make_async_copy(m_ref, slot, loc_sem.at[3])

    @pl.when(plane != z)
    def _():
        move2.start()

    @pl.when(plane == z)
    def _():
        move2_own.start()

    for c in a_x:
        c.wait()
    a_xy = fan(g_ref.at[y, :, core, lo], ay_s, ay_r, 3, at_y, 3)
    for c in a_xy:
        c.start()
    for c in a_y:
        c.wait()
    a_yx = fan(g_ref.at[:, x, core, hi], ax_s, ax_r, 3, at_x, 3)
    for c in a_yx:
        c.start()

    b_z = [copy(b_ref, br_ref.at[z], bz_s.at[k - 1], bz_r.at[k - 1], at_z(k))
           for k in range(1, COLS)]
    for c in b_z:
        c.start()

    def to_partner(ref, ssem, rsem, k):
        c = copy(ref, ref, ssem.at[k], rsem.at[k], partner)
        c.start()
        return c

    a_c = [to_partner(g_ref.at[y, :, core, lo], ac_s, ac_r, 0),
           to_partner(g_ref.at[:, x, core, hi], ac_s, ac_r, 4)]

    @pl.when(plane != z)
    def _():
        move2.wait()

    @pl.when(plane == z)
    def _():
        move2_own.wait()

    blo, bhi = pl.ds(0, 32), pl.ds(32, 32)
    b_x = fan(bc_ref.at[core, y, x, blo], bx_s, bx_r, 0, at_x, 3)
    b_y = fan(bc_ref.at[core, y, x, bhi], by_s, by_r, 0, at_y, 3)
    for p, q in zip(b_x, b_y):
        p.start()
        q.start()

    for k in range(1, 4):
        a_xy[k - 1].wait_recv()
        a_c.append(to_partner(g_ref.at[(y + 4 - k) % 4, :, core, lo], ac_s, ac_r, k))
        a_yx[k - 1].wait_recv()
        a_c.append(to_partner(g_ref.at[:, (x + 4 - k) % 4, core, hi], ac_s, ac_r, 4 + k))
    for c in a_xy + a_yx:
        c.wait_send()

    for c in b_x:
        c.wait()
    b_xy = fan(bc_ref.at[core, y, :, blo], by_s, by_r, 3, at_y, 3)
    for c in b_xy:
        c.start()
    for c in b_y:
        c.wait()
    b_yx = fan(bc_ref.at[core, :, x, bhi], bx_s, bx_r, 3, at_x, 3)
    for c in b_yx:
        c.start()
    for c in a_c:
        c.wait()

    for r in range(2 * CHIPS):
        for s in range(2):
            for l in range(4):
                a4_ref[l, pl.ds(16 * r + s, 8, stride=2), :] = (
                    g_ref[r // 8, r // 2 % 4, r % 2, :, 2 * l + s, :])
    for l in range(4):
        a_ref[:, l * 128:(l + 1) * 128] = a4_ref[l]

    b_c = []

    def between():
        b_c.append(to_partner(bc_ref.at[core, y, :, blo], bk_s, bk_r, 0))
        b_c.append(to_partner(bc_ref.at[core, :, x, bhi], bk_s, bk_r, 4))
        own_b.wait()
        for c in b_z:
            c.wait()
        bt_ref[...] = br_ref[...].reshape(512, 256).T
        for k in range(1, 4):
            b_xy[k - 1].wait()
            b_c.append(to_partner(bc_ref.at[core, (y + 4 - k) % 4, :, blo], bk_s, bk_r, k))
            b_yx[k - 1].wait()
            b_c.append(to_partner(bc_ref.at[core, :, (x + 4 - k) % 4, bhi], bk_s, bk_r, 4 + k))

    w11, w21, w22 = factor_inverse(a_ref, between)
    w_ref[0:256, 0:256] = w11
    w_ref[0:256, 256:512] = jnp.zeros((256, 256), F32)
    w_ref[256:512, 0:256] = w21
    w_ref[256:512, 256:512] = w22

    w1s = split(w11)
    w2s = split(jnp.concatenate([w21, w22], 1))
    d = row * COLS + z
    mine = split(a_ref[pl.ds(pl.multiple_of((d // 4) * 8, 8), 8), :])
    l_ref[:, 0:256] = dot3s([v[:, :256] for v in mine], w1s, NT)
    l_ref[:, 256:512] = dot3s(mine, w2s, NT)
    lane = lax.broadcasted_iota(jnp.int32, (1, 512), 1)
    for s in range(2):
        line_s = l_ref[pl.ds(2 * (d % 4) + s, 1), :]
        line_s = jnp.where(lane <= 2 * d + s, line_s, 0.0)
        for l in range(4):
            fd_ref[2 * l + s:2 * l + s + 1, :] = line_s[:, l * 128:(l + 1) * 128]

    fp_ref[...] = dot3(w_ref[pl.ds(pl.multiple_of(z * 64, 64), 64), :],
                       br_ref[...].reshape(512, 256))
    b_s = split(bt_ref[...])
    p1 = split(dot3s([v[:, :256] for v in b_s], w1s, NT))
    p2 = split(dot3s(b_s, w2s, NT))
    u2 = dot3s(p2, w2s)
    u1 = u2[:, :256] + dot3s(p1, w1s)
    for cols, u in ((slice(0, 256), u1), (slice(256, 512), u2[:, 256:])):
        uh_ref[:, cols], ul_ref[:, cols] = split(u)
    own_t.wait()
    for c in b_c:
        c.wait()


def step(d_tile, b_t, trailing):
    vmem = pl.BlockSpec(memory_space=pltpu.VMEM)
    hbm = pl.BlockSpec(memory_space=pltpu.HBM)
    dma = lambda n: [pltpu.SemaphoreType.DMA((n,))] * 2
    return pl.pallas_call(
        step_kernel,
        out_shape=(
            jax.ShapeDtypeStruct((2, 4, 4, 64, 256), F32),
            jax.ShapeDtypeStruct((8, 128), F32),
            jax.ShapeDtypeStruct((64, 256), F32),
            jax.ShapeDtypeStruct((256, 512), BF16),
            jax.ShapeDtypeStruct((256, 512), BF16),
            jax.ShapeDtypeStruct((256, 1024), F32),
        ),
        in_specs=[hbm] * 3,
        out_specs=(vmem,) * 6,
        scratch_shapes=[
            pltpu.VMEM((4, 4, 2, COLS, 8, 128), F32),
            pltpu.VMEM((COLS, 64, 256), F32),
            pltpu.VMEM((64, 256), F32),
            pltpu.VMEM((4, 512, 128), F32),
            pltpu.VMEM((512, 512), F32),
            pltpu.VMEM((512, 512), F32),
            pltpu.VMEM((8, 512), F32),
            pltpu.VMEM((256, 512), F32),
            *dma(7), *dma(6), *dma(6), *dma(8),
            *dma(7), *dma(2), *dma(6), *dma(6), *dma(8),
            pltpu.SemaphoreType.DMA((5,)),
        ],
        compiler_params=pltpu.CompilerParams(
            collective_id=0, has_side_effects=True, vmem_limit_bytes=40 * 1024 * 1024),
        name="step",
    )(*[pltpu.with_memory_space_constraint(v, pltpu.HBM) for v in (d_tile, b_t, trailing)])


def update_kernel(uh_ref, ul_ref, bc_ref, t_ref, fd_in, fp_in, s_ref, fd_ref, fp_ref,
                  out_ref, sem):
    z = lax.axis_index("col")
    u_s = (uh_ref[...], ul_ref[...])
    copies = []
    for q in range(4):
        b, core = q // 2, q % 2
        rows = jnp.concatenate([bc_ref[core, (k + z) % COLS, b] for k in range(COLS)], 0)
        cols = slice(q * 256, (q + 1) * 256)
        out_ref[q] = t_ref[:, cols] - dot3s(u_s, split(rows))
        copies.append(pltpu.make_async_copy(out_ref.at[q], s_ref.at[:, cols], sem.at[q]))
        copies[-1].start()
    fd_ref[...] = fd_in[...]
    fp_ref[...] = fp_in[...]
    for c in copies:
        c.wait()


def update(uh, ul, bc, trailing, fd, fp):
    vmem = pl.BlockSpec(memory_space=pltpu.VMEM)
    return pl.pallas_call(
        update_kernel,
        out_shape=(
            jax.ShapeDtypeStruct((256, 1024), F32),
            jax.ShapeDtypeStruct((8, 128), F32),
            jax.ShapeDtypeStruct((64, 256), F32),
        ),
        in_specs=[vmem] * 6,
        out_specs=(pl.BlockSpec(memory_space=pltpu.HBM), vmem, vmem),
        scratch_shapes=[pltpu.VMEM((4, 256, 256), F32), pltpu.SemaphoreType.DMA((4,))],
        compiler_params=pltpu.CompilerParams(vmem_limit_bytes=16 * 1024 * 1024),
        name="update",
    )(uh, ul, bc, trailing, fd, fp)


def per_device(diag_block, panel_block, trailing):
    tile = diag_block.reshape(2, 4, 128).transpose(1, 0, 2).reshape(8, 128)
    bc, fd, fp, uh, ul, t = step(tile, panel_block.T, trailing)
    schur, fd, fp = update(uh, ul, bc.reshape(2, COLS, 2, 64, 256), t, fd, fp)
    fd = fd.reshape(4, 2, 128).transpose(1, 0, 2).reshape(2, 512)
    return fd, fp.T, schur


def solution(mesh):
    return jax.shard_map(
        per_device,
        mesh=mesh,
        in_specs=(P(("row", "col"), None), P("row", "col"), P("row", "col")),
        out_specs=(P(("row", "col"), None), P("row", "col"), P("row", "col")),
        check_vma=False,
    )
```

```python
import functools

import jax
import jax.numpy as jnp
from jax import lax
from jax.experimental import pallas as pl
from jax.experimental.pallas import tpu as pltpu
from jax.sharding import PartitionSpec as P

NB = 512
F32 = jnp.float32
BF16 = jnp.bfloat16
MESH = pl.DeviceIdType.MESH
CHIPS = 16
COLS = 8


def split(x):
    high = x.astype(BF16)
    return high, (x - high.astype(F32)).astype(BF16)


def mm(a, b, dims):
    return lax.dot_general(a, b, (dims, ((), ())), preferred_element_type=F32)


NN = ((1,), (0,))
NT = ((1,), (1,))


def dot3s(a, b, dims=NN):
    return mm(a[0], b[0], dims) + (mm(a[0], b[1], dims) + mm(a[1], b[0], dims))


def dot3(a, b, dims=NN):
    return dot3s(split(a), split(b), dims)


def dotp(a, b):
    bh, bl = split(b)
    w = jnp.concatenate([bh, bl], 1)
    out = mm(jnp.concatenate(split(a), 1), jnp.concatenate([w, w], 0), NN)
    n = b.shape[1]
    return out[:, :n] + out[:, n:]


def dotp_t(a, b):
    bh, bl = split(b)
    w = jnp.concatenate([jnp.concatenate([bh, bh], 1), jnp.concatenate([bl, bl], 1)], 0)
    out = mm(jnp.concatenate(split(a), 1), w, NT)
    n = b.shape[0]
    return out[:, :n] + out[:, n:]


def scales(top, tol):
    e = (top - 1.0) / (top + 1.0)
    out = []
    while e > tol:
        m = 2.0 / (2.0 - e * e)
        out.append((m, e))
        e = e * e * m / 2.0
    return 2.0 / (1.0 + top), out


def grid2(n):
    i = lax.broadcasted_iota(jnp.int32, (n, n), 0)
    j = lax.broadcasted_iota(jnp.int32, (n, n), 1)
    return i, j


TOL = {256: 3e-4, 128: 1e-3, 64: 1e-3, 32: 1e-3, 16: 1e-3}
SMALL = 0.05
BASE = 32
GROUP = 4


def half_split(m, n, dot, dot_t):
    i, j = grid2(n)
    one = jnp.where(i == j, 1.0, 0.0)
    start, steps = scales(1.0 + n, TOL[n])
    zs = [start * x[:, :n] for x in m]
    for k, (s, e) in enumerate(steps):
        if e < SMALL:
            ns = [(s * (one - z[:n])).astype(BF16) for z in zs]
        else:
            ns = [(2.0 * s) * one - s * z[:n] for z in zs]
        if k == len(steps) - 1:
            zs = [z[n:] for z in zs]
        if e < SMALL:
            zs = [s * z + mm(z.astype(BF16), nn, NN) for z, nn in zip(zs, ns)]
        else:
            zs = [dot(z, nn) for z, nn in zip(zs, ns)]
    return zs, [x[n:, n:] - dot_t(z, x[n:, :n]) for x, z in zip(m, zs)]


def high_low(z, first):
    high = z.astype(BF16).astype(F32)
    out = jnp.where(first, high, z - high).astype(BF16)
    return jnp.concatenate([out, out], 1)


def twice(n, b):
    rows = []
    for k in range(0, 128, 2 * b):
        rows += [n[k:k + b]] * 2
    return jnp.concatenate(rows, 0)


def dot_pair(hl, n, b):
    high = n.astype(BF16).astype(F32)
    w = jnp.concatenate([twice(high, b).astype(BF16), twice(n - high, b).astype(BF16)], 0)
    return mm(hl, w, NN)


def tile_split(tiles, ts, b):
    i, j = grid2(128)
    bi, bj = i // b, j // b
    pair = i // (2 * b) == j // (2 * b)
    even = bi % 2 == 0
    first = bj % 2 == 0
    unit = jnp.where(jnp.logical_and(jnp.logical_and(pair, even), i % b == j % b), 1.0, 0.0)
    start, steps = scales(1.0 + b, TOL[b])
    doubled = [jnp.where(pair, jnp.where(first, m, pltpu.roll(m, b, 1)), 0.0) for m in tiles]
    zs = [start * d for d in doubled]
    for s, e in steps:
        if e < SMALL:
            ns = [jnp.where(even, s * (unit - z), 0.0).astype(BF16) for z in zs]
            zs = [s * z + mm(z.astype(BF16), nn, NN) for z, nn in zip(zs, ns)]
        else:
            ns = [(2.0 * s) * unit - s * z for z in zs]
            zs = [dot_pair(high_low(z, first), nn, b) for z, nn in zip(zs, ns)]
    gs = [high_low(jnp.where(even, 0.0, z), first) for z in zs]
    out = []
    for m, g, d in zip(tiles, gs, doubled):
        lows = split(jnp.where(even, 0.0, d))
        out.append(jnp.where(bi == bj, m, 0.0) - mm(g, jnp.concatenate(lows, 1), NT))
    if ts is None:
        g_only = [jnp.where(jnp.logical_and(first, jnp.logical_not(even)), z, 0.0) for z in zs]
        return out, [jnp.where(i == j, 1.0, 0.0) - g for g in g_only]
    return out, [t - dot_pair(g, t, b) for t, g in zip(ts, gs)]


def base_factors(tiles):
    sub = lax.broadcasted_iota(jnp.int32, (BASE, 128), 0)
    lane = lax.broadcasted_iota(jnp.int32, (BASE, 128), 1)
    groups = 128 // BASE
    rows = []
    for m in tiles:
        acc = None
        for g in range(groups):
            part = jnp.where(lane // BASE == g, m[g * BASE:(g + 1) * BASE], 0.0)
            acc = part if acc is None else acc + part
        rows.append(acc)
    ident = jnp.where(sub == lane % BASE, 1.0, 0.0)
    es = [ident] * len(tiles)
    for p0 in range(0, BASE, GROUP):
        index = [(lane // BASE) * BASE + p0 + c for c in range(GROUP)]
        for t in range(len(tiles)):
            cols = [jnp.take_along_axis(rows[t], i, axis=1, mode="promise_in_bounds")
                    for i in index]
            for c in range(GROUP):
                p = p0 + c
                root = lax.rsqrt(cols[c][p:p + 1])
                e_row = es[t][p:p + 1] * root
                if p == BASE - 1:
                    es[t] = jnp.where(sub == p, e_row, es[t])
                    break
                inv = root * root
                below = jnp.where(sub > p, cols[c], 0.0)
                for q in range(c + 1, GROUP):
                    cols[q] = cols[q] - below * (cols[q][p:p + 1] * inv)
                if p0 + GROUP < BASE:
                    rows[t] = rows[t] - below * (rows[t][p:p + 1] * inv)
                es[t] = jnp.where(sub == p, e_row, es[t] - below * (e_row * root))
    return [jnp.concatenate([jnp.where(lane // BASE == g, e, 0.0) for g in range(groups)], 0)
            for e in es]


def factor_inverse(a, between=lambda: None):
    (g1,), (s,) = half_split([a()], 256, dot3, lambda x, y: dot3(x, y, NT))
    blocks = [a()[:256, :256], s]
    g2, s2 = half_split(blocks, 128, dotp, dotp_t)
    tiles = [blocks[0][:128, :128], s2[0], blocks[1][:128, :128], s2[1]]
    ts = None
    b = 64
    while b >= BASE:
        tiles, ts = tile_split(tiles, ts, b)
        b //= 2
    g1p = jnp.concatenate([g1[:128], g1[128:] - dotp(g2[1], g1[:128])], 0)
    bases = base_factors(tiles)
    between()
    ts = [dotp(e, t) for e, t in zip(bases, ts)]
    zero = jnp.zeros((128, 128), F32)
    w11, w22 = [jnp.concatenate([
        jnp.concatenate([ts[2 * k], zero], 1),
        jnp.concatenate([-dotp(ts[2 * k + 1], g2[k]), ts[2 * k + 1]], 1)], 0) for k in range(2)]
    w21 = -jnp.concatenate([dotp(ts[2], g1p[:128]), dotp(ts[3], g1p[128:])], 0)

    i, j = grid2(256)
    one = jnp.where(i == j, 1.0, 0.0)
    low_half = jnp.where(i > j, 1.0, jnp.where(i == j, 0.5, 0.0))
    a_s = split(a())
    w1s = split(w11)
    w2s = split(jnp.concatenate([w21, w22], 1))
    wa1 = split(dot3s(w1s, [x[:256, :256] for x in a_s]))
    wa2 = split(dot3s(w2s, a_s))
    p11 = ((dot3s(wa1, w1s, NT) - one) * low_half).astype(BF16)
    p21 = dot3s([x[:, :256] for x in wa2], w1s, NT).astype(BF16)
    p22 = ((dot3s(wa2, w2s, NT) - one) * low_half).astype(BF16)
    n11 = w11 - mm(p11, w1s[0], NN)
    nw2 = mm(p22, w2s[0], NN)
    return n11, w21 - nw2[:, :256] - mm(p21, w1s[0], NN), w22 - nw2[:, 256:]


def step_kernel(d_ref, b_ref, t_ref, bc_ref, fd_ref, fp_ref, uh_ref, ul_ref, to_ref,
                g_ref, br_ref, m_ref, a4_ref, p_ref, bt_ref,
                az_s, az_r, ax_s, ax_r, ay_s, ay_r, ac_s, ac_r,
                bz_s, bz_r, mv_s, mv_r, bx_s, bx_r, by_s, by_r, bk_s, bk_r, loc_sem):
    row = lax.axis_index("row")
    z = lax.axis_index("col")
    chip = row // 2
    core = row % 2
    y = chip // 4
    x = chip % 4

    def at_z(k):
        return {"row": row, "col": (z + k) % COLS}

    def at_chip(k):
        return {"row": ((chip + k) % CHIPS) * 2 + core, "col": z}

    def at_x(k):
        return {"row": (y * 4 + (x + k) % 4) * 2 + core, "col": z}

    def at_y(k):
        return {"row": (((y + k) % 4) * 4 + x) * 2 + core, "col": z}

    partner = {"row": row + 1 - 2 * core, "col": z}

    def copy(src, dst, ssem, rsem, device):
        return pltpu.make_async_remote_copy(
            src_ref=src, dst_ref=dst, send_sem=ssem, recv_sem=rsem,
            device_id=device, device_id_type=MESH)

    def fan(ref, ssem, rsem, first, where, n):
        return [copy(ref, ref, ssem.at[first + k - 1], rsem.at[first + k - 1], where(k))
                for k in range(1, n + 1)]

    barrier = pltpu.get_barrier_semaphore()
    for k in range(1, COLS):
        pl.semaphore_signal(barrier, inc=1, device_id=at_z(k), device_id_type=MESH)
    for k in range(1, CHIPS):
        pl.semaphore_signal(barrier, inc=1, device_id=at_chip(k), device_id_type=MESH)
    pl.semaphore_signal(barrier, inc=1, device_id=partner, device_id_type=MESH)
    own_tile = g_ref.at[y, x, core, z]
    own_a = pltpu.make_async_copy(d_ref, own_tile, loc_sem.at[0])
    own_b = pltpu.make_async_copy(b_ref, br_ref.at[z], loc_sem.at[1])
    own_t = pltpu.make_async_copy(t_ref, to_ref, loc_sem.at[4])
    own_a.start()
    own_b.start()
    pl.semaphore_wait(barrier, COLS + CHIPS - 1)

    a_z = [copy(d_ref, own_tile, az_s.at[k - 1], az_r.at[k - 1], at_z(k))
           for k in range(1, COLS)]
    for c in a_z:
        c.start()

    move1 = copy(b_ref, m_ref, mv_s.at[0], mv_r.at[0], at_chip(2 * z))
    move1_own = pltpu.make_async_copy(b_ref, m_ref, loc_sem.at[2])

    @pl.when(z != 0)
    def _():
        move1.start()

    @pl.when(z == 0)
    def _():
        move1_own.start()

    own_t.start()
    own_a.wait()
    for c in a_z:
        c.wait()

    lo, hi = pl.ds(0, 4), pl.ds(4, 4)
    a_x = fan(g_ref.at[y, x, core, lo], ax_s, ax_r, 0, at_x, 3)
    a_y = fan(g_ref.at[y, x, core, hi], ay_s, ay_r, 0, at_y, 3)
    for p, q in zip(a_x, a_y):
        p.start()
        q.start()

    @pl.when(z != 0)
    def _():
        move1.wait()

    @pl.when(z == 0)
    def _():
        move1_own.wait()

    src = (chip + CHIPS - 2 * z) % CHIPS
    plane = src // 2
    slot = bc_ref.at[core, y, x]
    move2 = copy(m_ref, slot, mv_s.at[1], mv_r.at[1], {"row": row, "col": plane})
    move2_own = pltpu.make_async_copy(m_ref, slot, loc_sem.at[3])

    @pl.when(plane != z)
    def _():
        move2.start()

    @pl.when(plane == z)
    def _():
        move2_own.start()

    for c in a_x:
        c.wait()
    a_xy = fan(g_ref.at[y, :, core, lo], ay_s, ay_r, 3, at_y, 3)
    for c in a_xy:
        c.start()
    for c in a_y:
        c.wait()
    a_yx = fan(g_ref.at[:, x, core, hi], ax_s, ax_r, 3, at_x, 3)
    for c in a_yx:
        c.start()

    b_z = [copy(b_ref, br_ref.at[z], bz_s.at[k - 1], bz_r.at[k - 1], at_z(k))
           for k in range(1, COLS)]
    for c in b_z:
        c.start()

    def to_partner(ref, ssem, rsem, k):
        c = copy(ref, ref, ssem.at[k], rsem.at[k], partner)
        c.start()
        return c

    a_c = [to_partner(g_ref.at[y, :, core, lo], ac_s, ac_r, 0),
           to_partner(g_ref.at[:, x, core, hi], ac_s, ac_r, 4)]

    @pl.when(plane != z)
    def _():
        move2.wait()

    @pl.when(plane == z)
    def _():
        move2_own.wait()

    blo, bhi = pl.ds(0, 32), pl.ds(32, 32)
    b_x = fan(bc_ref.at[core, y, x, blo], bx_s, bx_r, 0, at_x, 3)
    b_y = fan(bc_ref.at[core, y, x, bhi], by_s, by_r, 0, at_y, 3)
    for p, q in zip(b_x, b_y):
        p.start()
        q.start()

    for k in range(1, 4):
        a_xy[k - 1].wait_recv()
        a_c.append(to_partner(g_ref.at[(y + 4 - k) % 4, :, core, lo], ac_s, ac_r, k))
        a_yx[k - 1].wait_recv()
        a_c.append(to_partner(g_ref.at[:, (x + 4 - k) % 4, core, hi], ac_s, ac_r, 4 + k))
    for c in a_xy + a_yx:
        c.wait_send()

    for c in b_x:
        c.wait()
    b_xy = fan(bc_ref.at[core, y, :, blo], by_s, by_r, 3, at_y, 3)
    for c in b_xy:
        c.start()
    for c in b_y:
        c.wait()
    b_yx = fan(bc_ref.at[core, :, x, bhi], bx_s, bx_r, 3, at_x, 3)
    for c in b_yx:
        c.start()
    def place(k):
        for c in range(CHIPS):
            for s in range(2):
                for l in range(4):
                    a4_ref[l, pl.ds(32 * c + 16 * k + s, 8, stride=2), :] = (
                        g_ref[c // 4, c % 4, k, :, 2 * l + s, :])

    place(core)
    for c in a_c:
        c.wait()
    place(1 - core)

    def block():
        return jnp.concatenate([a4_ref[l] for l in range(4)], 1)

    b_c = []

    def between():
        b_c.append(to_partner(bc_ref.at[core, y, :, blo], bk_s, bk_r, 0))
        b_c.append(to_partner(bc_ref.at[core, :, x, bhi], bk_s, bk_r, 4))
        own_b.wait()
        for c in b_z:
            c.wait()
        bt_ref[...] = br_ref[...].reshape(512, 256).T
        for k in range(1, 4):
            b_xy[k - 1].wait()
            b_c.append(to_partner(bc_ref.at[core, (y + 4 - k) % 4, :, blo], bk_s, bk_r, k))
            b_yx[k - 1].wait()
            b_c.append(to_partner(bc_ref.at[core, :, (x + 4 - k) % 4, bhi], bk_s, bk_r, 4 + k))

    w11, w21, w22 = factor_inverse(block, between)
    w1s = split(w11)
    w2s = split(jnp.concatenate([w21, w22], 1))
    d = row * COLS + z
    sixteen = pl.ds(pl.multiple_of((d // 8) * 16, 16), 16)
    mine = split(jnp.concatenate([a4_ref[l, sixteen, :] for l in range(4)], 1))
    b_s = [jnp.concatenate(v, 0) for v in zip(split(bt_ref[...]), mine)]
    p1 = dot3s([v[:, :256] for v in b_s], w1s, NT)
    p2 = dot3s(b_s, w2s, NT)
    p_ref[:, 0:256] = p1
    p_ref[:, 256:512] = p2
    p2s = split(p2[:256])
    u2 = dot3s(p2s, w2s)
    u1 = u2[:, :256] + dot3s(split(p1[:256]), w1s)
    for cols, u in ((slice(0, 256), u1), (slice(256, 512), u2[:, 256:])):
        uh_ref[:, cols], ul_ref[:, cols] = split(u)
    lane = lax.broadcasted_iota(jnp.int32, (1, 512), 1)
    for s in range(2):
        line_s = p_ref[pl.ds(256 + 2 * (d % 8) + s, 1), :]
        line_s = jnp.where(lane <= 2 * d + s, line_s, 0.0)
        for l in range(4):
            fd_ref[2 * l + s:2 * l + s + 1, :] = line_s[:, l * 128:(l + 1) * 128]
    part = p_ref[0:256, pl.ds(pl.multiple_of((z // 2) * 128, 128), 128)].T
    fp_ref[...] = jnp.where(z % 2 == 0, part[:64], part[64:])
    own_t.wait()
    for c in b_c:
        c.wait()


def step(d_tile, b_t, trailing):
    vmem = pl.BlockSpec(memory_space=pltpu.VMEM)
    hbm = pl.BlockSpec(memory_space=pltpu.HBM)
    dma = lambda n: [pltpu.SemaphoreType.DMA((n,))] * 2
    return pl.pallas_call(
        step_kernel,
        out_shape=(
            jax.ShapeDtypeStruct((2, 4, 4, 64, 256), F32),
            jax.ShapeDtypeStruct((8, 128), F32),
            jax.ShapeDtypeStruct((64, 256), F32),
            jax.ShapeDtypeStruct((256, 512), BF16),
            jax.ShapeDtypeStruct((256, 512), BF16),
            jax.ShapeDtypeStruct((256, 1024), F32),
        ),
        in_specs=[hbm] * 3,
        out_specs=(vmem,) * 6,
        scratch_shapes=[
            pltpu.VMEM((4, 4, 2, COLS, 8, 128), F32),
            pltpu.VMEM((COLS, 64, 256), F32),
            pltpu.VMEM((64, 256), F32),
            pltpu.VMEM((4, 512, 128), F32),
            pltpu.VMEM((272, 512), F32),
            pltpu.VMEM((256, 512), F32),
            *dma(7), *dma(6), *dma(6), *dma(8),
            *dma(7), *dma(2), *dma(6), *dma(6), *dma(8),
            pltpu.SemaphoreType.DMA((5,)),
        ],
        compiler_params=pltpu.CompilerParams(
            collective_id=0, has_side_effects=True, vmem_limit_bytes=40 * 1024 * 1024),
        name="step",
    )(*[pltpu.with_memory_space_constraint(v, pltpu.HBM) for v in (d_tile, b_t, trailing)])


def update_kernel(uh_ref, ul_ref, bc_ref, t_ref, fd_in, fp_in, s_ref, fd_ref, fp_ref,
                  out_ref, sem):
    z = lax.axis_index("col")
    u_s = (uh_ref[...], ul_ref[...])
    copies = []
    for q in range(4):
        b, core = q // 2, q % 2
        rows = jnp.concatenate([bc_ref[core, (k + z) % COLS, b] for k in range(COLS)], 0)
        cols = slice(q * 256, (q + 1) * 256)
        out_ref[q] = t_ref[:, cols] - dot3s(u_s, split(rows))
        copies.append(pltpu.make_async_copy(out_ref.at[q], s_ref.at[:, cols], sem.at[q]))
        copies[-1].start()
    fd_ref[...] = fd_in[...]
    fp_ref[...] = fp_in[...]
    for c in copies:
        c.wait()


def update(uh, ul, bc, trailing, fd, fp):
    vmem = pl.BlockSpec(memory_space=pltpu.VMEM)
    return pl.pallas_call(
        update_kernel,
        out_shape=(
            jax.ShapeDtypeStruct((256, 1024), F32),
            jax.ShapeDtypeStruct((8, 128), F32),
            jax.ShapeDtypeStruct((64, 256), F32),
        ),
        in_specs=[vmem] * 6,
        out_specs=(pl.BlockSpec(memory_space=pltpu.HBM), vmem, vmem),
        scratch_shapes=[pltpu.VMEM((4, 256, 256), F32), pltpu.SemaphoreType.DMA((4,))],
        compiler_params=pltpu.CompilerParams(vmem_limit_bytes=16 * 1024 * 1024),
        name="update",
    )(uh, ul, bc, trailing, fd, fp)


def per_device(diag_block, panel_block, trailing):
    tile = diag_block.reshape(2, 4, 128).transpose(1, 0, 2).reshape(8, 128)
    bc, fd, fp, uh, ul, t = step(tile, panel_block.T, trailing)
    schur, fd, fp = update(uh, ul, bc.reshape(2, COLS, 2, 64, 256), t, fd, fp)
    fd = fd.reshape(4, 2, 128).transpose(1, 0, 2).reshape(2, 512)
    return fd, fp.T, schur


def solution(mesh):
    return jax.shard_map(
        per_device,
        mesh=mesh,
        in_specs=(P(("row", "col"), None), P("row", "col"), P("row", "col")),
        out_specs=(P(("row", "col"), None), P("row", "col"), P("row", "col")),
        check_vma=False,
    )
```

```python
import functools

import jax
import jax.numpy as jnp
from jax import lax
from jax.experimental import pallas as pl
from jax.experimental.pallas import tpu as pltpu
from jax.sharding import PartitionSpec as P

NB = 512
F32 = jnp.float32
BF16 = jnp.bfloat16
MESH = pl.DeviceIdType.MESH
CHIPS = 16
COLS = 8


def split(x):
    high = x.astype(BF16)
    return high, (x - high.astype(F32)).astype(BF16)


def mm(a, b, dims):
    return lax.dot_general(a, b, (dims, ((), ())), preferred_element_type=F32)


NN = ((1,), (0,))
NT = ((1,), (1,))


def dot3s(a, b, dims=NN):
    return mm(a[0], b[0], dims) + (mm(a[0], b[1], dims) + mm(a[1], b[0], dims))


def dot3(a, b, dims=NN):
    return dot3s(split(a), split(b), dims)


def dotp(a, b):
    bh, bl = split(b)
    w = jnp.concatenate([bh, bl], 1)
    out = mm(jnp.concatenate(split(a), 1), jnp.concatenate([w, w], 0), NN)
    n = b.shape[1]
    return out[:, :n] + out[:, n:]


def dotp_t(a, b):
    bh, bl = split(b)
    w = jnp.concatenate([jnp.concatenate([bh, bh], 1), jnp.concatenate([bl, bl], 1)], 0)
    out = mm(jnp.concatenate(split(a), 1), w, NT)
    n = b.shape[0]
    return out[:, :n] + out[:, n:]


def scales(top, tol):
    e = (top - 1.0) / (top + 1.0)
    out = []
    while e > tol:
        m = 2.0 / (2.0 - e * e)
        out.append((m, e))
        e = e * e * m / 2.0
    return 2.0 / (1.0 + top), out


def grid2(n):
    i = lax.broadcasted_iota(jnp.int32, (n, n), 0)
    j = lax.broadcasted_iota(jnp.int32, (n, n), 1)
    return i, j


TOL = {256: 3e-4, 128: 1e-3, 64: 1e-3, 32: 1e-3, 16: 1e-3}
SMALL = 0.15
BASE = 32
GROUP = 4


def half_split(m, n, dot, dot_t):
    i, j = grid2(n)
    one = jnp.where(i == j, 1.0, 0.0)
    start, steps = scales(1.0 + n, TOL[n])
    zs = [start * x[:, :n] for x in m]
    for k, (s, e) in enumerate(steps):
        if e < SMALL:
            ns = [(s * (one - z[:n])).astype(BF16) for z in zs]
        else:
            ns = [(2.0 * s) * one - s * z[:n] for z in zs]
        if k == len(steps) - 1:
            zs = [z[n:] for z in zs]
        if e < SMALL:
            zs = [s * z + mm(z.astype(BF16), nn, NN) for z, nn in zip(zs, ns)]
        else:
            zs = [dot(z, nn) for z, nn in zip(zs, ns)]
    return zs, [x[n:, n:] - dot_t(z, x[n:, :n]) for x, z in zip(m, zs)]


def high_low(z, first):
    high = z.astype(BF16).astype(F32)
    out = jnp.where(first, high, z - high).astype(BF16)
    return jnp.concatenate([out, out], 1)


def twice(n, b):
    rows = []
    for k in range(0, 128, 2 * b):
        rows += [n[k:k + b]] * 2
    return jnp.concatenate(rows, 0)


def dot_pair(hl, n, b):
    high = n.astype(BF16).astype(F32)
    w = jnp.concatenate([twice(high, b).astype(BF16), twice(n - high, b).astype(BF16)], 0)
    return mm(hl, w, NN)


def tile_split(tiles, ts, b):
    i, j = grid2(128)
    bi, bj = i // b, j // b
    pair = i // (2 * b) == j // (2 * b)
    even = bi % 2 == 0
    first = bj % 2 == 0
    unit = jnp.where(jnp.logical_and(jnp.logical_and(pair, even), i % b == j % b), 1.0, 0.0)
    start, steps = scales(1.0 + b, TOL[b])
    doubled = [jnp.where(pair, jnp.where(first, m, pltpu.roll(m, b, 1)), 0.0) for m in tiles]
    zs = [start * d for d in doubled]
    for s, e in steps:
        if e < SMALL:
            ns = [jnp.where(even, s * (unit - z), 0.0).astype(BF16) for z in zs]
            zs = [s * z + mm(z.astype(BF16), nn, NN) for z, nn in zip(zs, ns)]
        else:
            ns = [(2.0 * s) * unit - s * z for z in zs]
            zs = [dot_pair(high_low(z, first), nn, b) for z, nn in zip(zs, ns)]
    gs = [high_low(jnp.where(even, 0.0, z), first) for z in zs]
    out = []
    for m, g, d in zip(tiles, gs, doubled):
        lows = split(jnp.where(even, 0.0, d))
        out.append(jnp.where(bi == bj, m, 0.0) - mm(g, jnp.concatenate(lows, 1), NT))
    if ts is None:
        g_only = [jnp.where(jnp.logical_and(first, jnp.logical_not(even)), z, 0.0) for z in zs]
        return out, [jnp.where(i == j, 1.0, 0.0) - g for g in g_only]
    return out, [t - dot_pair(g, t, b) for t, g in zip(ts, gs)]


def base_factors(tiles):
    sub = lax.broadcasted_iota(jnp.int32, (BASE, 128), 0)
    lane = lax.broadcasted_iota(jnp.int32, (BASE, 128), 1)
    groups = 128 // BASE
    rows = []
    for m in tiles:
        acc = None
        for g in range(groups):
            part = jnp.where(lane // BASE == g, m[g * BASE:(g + 1) * BASE], 0.0)
            acc = part if acc is None else acc + part
        rows.append(acc)
    ident = jnp.where(sub == lane % BASE, 1.0, 0.0)
    es = [ident] * len(tiles)
    for p0 in range(0, BASE, GROUP):
        index = [(lane // BASE) * BASE + p0 + c for c in range(GROUP)]
        for t in range(len(tiles)):
            cols = [jnp.take_along_axis(rows[t], i, axis=1, mode="promise_in_bounds")
                    for i in index]
            for c in range(GROUP):
                p = p0 + c
                root = lax.rsqrt(cols[c][p:p + 1])
                e_row = es[t][p:p + 1] * root
                if p == BASE - 1:
                    es[t] = jnp.where(sub == p, e_row, es[t])
                    break
                inv = root * root
                below = jnp.where(sub > p, cols[c], 0.0)
                for q in range(c + 1, GROUP):
                    cols[q] = cols[q] - below * (cols[q][p:p + 1] * inv)
                if p0 + GROUP < BASE:
                    rows[t] = rows[t] - below * (rows[t][p:p + 1] * inv)
                es[t] = jnp.where(sub == p, e_row, es[t] - below * (e_row * root))
    return [jnp.concatenate([jnp.where(lane // BASE == g, e, 0.0) for g in range(groups)], 0)
            for e in es]


def factor_inverse(a, between=lambda: None):
    (g1,), (s,) = half_split([a()], 256, dot3, lambda x, y: dot3(x, y, NT))
    blocks = [a()[:256, :256], s]
    g2, s2 = half_split(blocks, 128, dotp, dotp_t)
    tiles = [blocks[0][:128, :128], s2[0], blocks[1][:128, :128], s2[1]]
    ts = None
    b = 64
    while b >= BASE:
        tiles, ts = tile_split(tiles, ts, b)
        b //= 2
    g1p = jnp.concatenate([g1[:128], g1[128:] - dotp(g2[1], g1[:128])], 0)
    bases = base_factors(tiles)
    between()
    ts = [dotp(e, t) for e, t in zip(bases, ts)]
    zero = jnp.zeros((128, 128), F32)
    w11, w22 = [jnp.concatenate([
        jnp.concatenate([ts[2 * k], zero], 1),
        jnp.concatenate([-dotp(ts[2 * k + 1], g2[k]), ts[2 * k + 1]], 1)], 0) for k in range(2)]
    w21 = -jnp.concatenate([dotp(ts[2], g1p[:128]), dotp(ts[3], g1p[128:])], 0)

    i, j = grid2(256)
    one = jnp.where(i == j, 1.0, 0.0)
    low_half = jnp.where(i > j, 1.0, jnp.where(i == j, 0.5, 0.0))
    a_s = split(a())
    w1s = split(w11)
    w2s = split(jnp.concatenate([w21, w22], 1))
    wa1 = split(dot3s(w1s, [x[:256, :256] for x in a_s]))
    wa2 = split(dot3s(w2s, a_s))
    p11 = ((dot3s(wa1, w1s, NT) - one) * low_half).astype(BF16)
    p21 = dot3s([x[:, :256] for x in wa2], w1s, NT).astype(BF16)
    p22 = ((dot3s(wa2, w2s, NT) - one) * low_half).astype(BF16)
    n11 = w11 - mm(p11, w1s[0], NN)
    nw2 = mm(p22, w2s[0], NN)
    return n11, w21 - nw2[:, :256] - mm(p21, w1s[0], NN), w22 - nw2[:, 256:]


def step_kernel(d_ref, b_ref, t_ref, bc_ref, fd_ref, fp_ref, uh_ref, ul_ref, to_ref,
                g_ref, br_ref, m_ref, a4_ref, p_ref, bt_ref,
                az_s, az_r, ax_s, ax_r, ay_s, ay_r, ac_s, ac_r,
                bz_s, bz_r, mv_s, mv_r, bx_s, bx_r, by_s, by_r, bk_s, bk_r, loc_sem):
    row = lax.axis_index("row")
    z = lax.axis_index("col")
    chip = row // 2
    core = row % 2
    y = chip // 4
    x = chip % 4

    def at_z(k):
        return {"row": row, "col": (z + k) % COLS}

    def at_chip(k):
        return {"row": ((chip + k) % CHIPS) * 2 + core, "col": z}

    def at_x(k):
        return {"row": (y * 4 + (x + k) % 4) * 2 + core, "col": z}

    def at_y(k):
        return {"row": (((y + k) % 4) * 4 + x) * 2 + core, "col": z}

    partner = {"row": row + 1 - 2 * core, "col": z}

    def copy(src, dst, ssem, rsem, device):
        return pltpu.make_async_remote_copy(
            src_ref=src, dst_ref=dst, send_sem=ssem, recv_sem=rsem,
            device_id=device, device_id_type=MESH)

    def fan(ref, ssem, rsem, first, where, n):
        return [copy(ref, ref, ssem.at[first + k - 1], rsem.at[first + k - 1], where(k))
                for k in range(1, n + 1)]

    barrier = pltpu.get_barrier_semaphore()
    for k in (4, 3, 5, 2, 6, 1, 7):
        pl.semaphore_signal(barrier, inc=1, device_id=at_z(k), device_id_type=MESH)
    for k in range(1, CHIPS):
        pl.semaphore_signal(barrier, inc=1, device_id=at_chip(k), device_id_type=MESH)
    pl.semaphore_signal(barrier, inc=1, device_id=partner, device_id_type=MESH)
    own_tile = g_ref.at[y, x, core, z]
    own_a = pltpu.make_async_copy(d_ref, own_tile, loc_sem.at[0])
    own_b = pltpu.make_async_copy(b_ref, br_ref.at[z], loc_sem.at[1])
    own_t = pltpu.make_async_copy(t_ref, to_ref, loc_sem.at[4])
    own_a.start()
    own_b.start()
    pl.semaphore_wait(barrier, COLS + CHIPS - 1)

    a_z = [copy(d_ref, own_tile, az_s.at[k - 1], az_r.at[k - 1], at_z(k))
           for k in range(1, COLS)]
    for k in (4, 3, 5, 2, 6, 1, 7):
        a_z[k - 1].start()

    move1 = copy(b_ref, m_ref, mv_s.at[0], mv_r.at[0], at_chip(2 * z))
    move1_own = pltpu.make_async_copy(b_ref, m_ref, loc_sem.at[2])

    @pl.when(z != 0)
    def _():
        move1.start()

    @pl.when(z == 0)
    def _():
        move1_own.start()

    own_t.start()
    own_a.wait()
    for c in a_z:
        c.wait()

    lo, hi = pl.ds(0, 4), pl.ds(4, 4)
    a_x = fan(g_ref.at[y, x, core, lo], ax_s, ax_r, 0, at_x, 3)
    a_y = fan(g_ref.at[y, x, core, hi], ay_s, ay_r, 0, at_y, 3)
    for k in (1, 0, 2):
        a_x[k].start()
        a_y[k].start()

    @pl.when(z != 0)
    def _():
        move1.wait()

    @pl.when(z == 0)
    def _():
        move1_own.wait()

    src = (chip + CHIPS - 2 * z) % CHIPS
    plane = src // 2
    slot = bc_ref.at[core, y, x]
    move2 = copy(m_ref, slot, mv_s.at[1], mv_r.at[1], {"row": row, "col": plane})
    move2_own = pltpu.make_async_copy(m_ref, slot, loc_sem.at[3])

    @pl.when(plane != z)
    def _():
        move2.start()

    @pl.when(plane == z)
    def _():
        move2_own.start()

    for c in a_x:
        c.wait()
    a_xy = fan(g_ref.at[y, :, core, lo], ay_s, ay_r, 3, at_y, 3)
    for k in (1, 0, 2):
        a_xy[k].start()
    for c in a_y:
        c.wait()
    a_yx = fan(g_ref.at[:, x, core, hi], ax_s, ax_r, 3, at_x, 3)
    for k in (1, 0, 2):
        a_yx[k].start()

    def to_partner(ref, ssem, rsem, k):
        c = copy(ref, ref, ssem.at[k], rsem.at[k], partner)
        c.start()
        return c

    a_c = [to_partner(g_ref.at[y, :, core, lo], ac_s, ac_r, 0),
           to_partner(g_ref.at[:, x, core, hi], ac_s, ac_r, 4)]

    @pl.when(plane != z)
    def _():
        move2.wait()

    @pl.when(plane == z)
    def _():
        move2_own.wait()

    blo, bhi = pl.ds(0, 32), pl.ds(32, 32)
    b_x = fan(bc_ref.at[core, y, x, blo], bx_s, bx_r, 0, at_x, 3)
    b_y = fan(bc_ref.at[core, y, x, bhi], by_s, by_r, 0, at_y, 3)
    for p, q in zip(b_x, b_y):
        p.start()
        q.start()

    b_z = [copy(b_ref, br_ref.at[z], bz_s.at[k - 1], bz_r.at[k - 1], at_z(k))
           for k in range(1, COLS)]
    for c in b_z:
        c.start()

    for k in range(1, 4):
        a_xy[k - 1].wait_recv()
        a_c.append(to_partner(g_ref.at[(y + 4 - k) % 4, :, core, lo], ac_s, ac_r, k))
        a_yx[k - 1].wait_recv()
        a_c.append(to_partner(g_ref.at[:, (x + 4 - k) % 4, core, hi], ac_s, ac_r, 4 + k))
    for c in a_xy + a_yx:
        c.wait_send()

    for c in b_x:
        c.wait()
    b_xy = fan(bc_ref.at[core, y, :, blo], by_s, by_r, 3, at_y, 3)
    for c in b_xy:
        c.start()
    for c in b_y:
        c.wait()
    b_yx = fan(bc_ref.at[core, :, x, bhi], bx_s, bx_r, 3, at_x, 3)
    for c in b_yx:
        c.start()
    def place(k):
        for c in range(CHIPS):
            for s in range(2):
                for l in range(4):
                    a4_ref[l, pl.ds(32 * c + 16 * k + s, 8, stride=2), :] = (
                        g_ref[c // 4, c % 4, k, :, 2 * l + s, :])

    place(core)
    for c in a_c:
        c.wait()
    place(1 - core)

    def block():
        return jnp.concatenate([a4_ref[l] for l in range(4)], 1)

    b_c = []

    def between():
        b_c.append(to_partner(bc_ref.at[core, y, :, blo], bk_s, bk_r, 0))
        b_c.append(to_partner(bc_ref.at[core, :, x, bhi], bk_s, bk_r, 4))
        own_b.wait()
        for c in b_z:
            c.wait()
        bt_ref[...] = br_ref[...].reshape(512, 256).T
        for k in range(1, 4):
            b_xy[k - 1].wait()
            b_c.append(to_partner(bc_ref.at[core, (y + 4 - k) % 4, :, blo], bk_s, bk_r, k))
            b_yx[k - 1].wait()
            b_c.append(to_partner(bc_ref.at[core, :, (x + 4 - k) % 4, bhi], bk_s, bk_r, 4 + k))

    w11, w21, w22 = factor_inverse(block, between)
    w1s = split(w11)
    w2s = split(jnp.concatenate([w21, w22], 1))
    d = row * COLS + z
    sixteen = pl.ds(pl.multiple_of((d // 8) * 16, 16), 16)
    mine = split(jnp.concatenate([a4_ref[l, sixteen, :] for l in range(4)], 1))
    b_s = [jnp.concatenate(v, 0) for v in zip(split(bt_ref[...]), mine)]
    p1 = dot3s([v[:, :256] for v in b_s], w1s, NT)
    p2 = dot3s(b_s, w2s, NT)
    p_ref[:, 0:256] = p1
    p_ref[:, 256:512] = p2
    p2s = split(p2[:256])
    u2 = dot3s(p2s, w2s)
    u1 = u2[:, :256] + dot3s(split(p1[:256]), w1s)
    for cols, u in ((slice(0, 256), u1), (slice(256, 512), u2[:, 256:])):
        uh_ref[:, cols], ul_ref[:, cols] = split(u)
    lane = lax.broadcasted_iota(jnp.int32, (1, 512), 1)
    for s in range(2):
        line_s = p_ref[pl.ds(256 + 2 * (d % 8) + s, 1), :]
        line_s = jnp.where(lane <= 2 * d + s, line_s, 0.0)
        for l in range(4):
            fd_ref[2 * l + s:2 * l + s + 1, :] = line_s[:, l * 128:(l + 1) * 128]
    part = p_ref[0:256, pl.ds(pl.multiple_of((z // 2) * 128, 128), 128)].T
    fp_ref[...] = jnp.where(z % 2 == 0, part[:64], part[64:])
    own_t.wait()
    for c in b_c:
        c.wait()


def step(d_tile, b_t, trailing):
    vmem = pl.BlockSpec(memory_space=pltpu.VMEM)
    hbm = pl.BlockSpec(memory_space=pltpu.HBM)
    dma = lambda n: [pltpu.SemaphoreType.DMA((n,))] * 2
    return pl.pallas_call(
        step_kernel,
        out_shape=(
            jax.ShapeDtypeStruct((2, 4, 4, 64, 256), F32),
            jax.ShapeDtypeStruct((8, 128), F32),
            jax.ShapeDtypeStruct((64, 256), F32),
            jax.ShapeDtypeStruct((256, 512), BF16),
            jax.ShapeDtypeStruct((256, 512), BF16),
            jax.ShapeDtypeStruct((256, 1024), F32),
        ),
        in_specs=[hbm] * 3,
        out_specs=(vmem,) * 6,
        scratch_shapes=[
            pltpu.VMEM((4, 4, 2, COLS, 8, 128), F32),
            pltpu.VMEM((COLS, 64, 256), F32),
            pltpu.VMEM((64, 256), F32),
            pltpu.VMEM((4, 512, 128), F32),
            pltpu.VMEM((272, 512), F32),
            pltpu.VMEM((256, 512), F32),
            *dma(7), *dma(6), *dma(6), *dma(8),
            *dma(7), *dma(2), *dma(6), *dma(6), *dma(8),
            pltpu.SemaphoreType.DMA((5,)),
        ],
        compiler_params=pltpu.CompilerParams(
            collective_id=0, has_side_effects=True, vmem_limit_bytes=40 * 1024 * 1024),
        name="step",
    )(*[pltpu.with_memory_space_constraint(v, pltpu.HBM) for v in (d_tile, b_t, trailing)])


def update_kernel(uh_ref, ul_ref, bc_ref, t_ref, fd_in, fp_in, s_ref, fd_ref, fp_ref,
                  out_ref, sem):
    z = lax.axis_index("col")
    u_s = (uh_ref[...], ul_ref[...])
    copies = []
    for q in range(4):
        b, core = q // 2, q % 2
        rows = jnp.concatenate([bc_ref[core, (k + z) % COLS, b] for k in range(COLS)], 0)
        cols = slice(q * 256, (q + 1) * 256)
        out_ref[q] = t_ref[:, cols] - dot3s(u_s, split(rows))
        copies.append(pltpu.make_async_copy(out_ref.at[q], s_ref.at[:, cols], sem.at[q]))
        copies[-1].start()
    fd_ref[...] = fd_in[...]
    fp_ref[...] = fp_in[...]
    for c in copies:
        c.wait()


def update(uh, ul, bc, trailing, fd, fp):
    vmem = pl.BlockSpec(memory_space=pltpu.VMEM)
    return pl.pallas_call(
        update_kernel,
        out_shape=(
            jax.ShapeDtypeStruct((256, 1024), F32),
            jax.ShapeDtypeStruct((8, 128), F32),
            jax.ShapeDtypeStruct((64, 256), F32),
        ),
        in_specs=[vmem] * 6,
        out_specs=(pl.BlockSpec(memory_space=pltpu.HBM), vmem, vmem),
        scratch_shapes=[pltpu.VMEM((4, 256, 256), F32), pltpu.SemaphoreType.DMA((4,))],
        compiler_params=pltpu.CompilerParams(vmem_limit_bytes=16 * 1024 * 1024),
        name="update",
    )(uh, ul, bc, trailing, fd, fp)


def per_device(diag_block, panel_block, trailing):
    tile = diag_block.reshape(2, 4, 128).transpose(1, 0, 2).reshape(8, 128)
    bc, fd, fp, uh, ul, t = step(tile, panel_block.T, trailing)
    schur, fd, fp = update(uh, ul, bc.reshape(2, COLS, 2, 64, 256), t, fd, fp)
    fd = fd.reshape(4, 2, 128).transpose(1, 0, 2).reshape(2, 512)
    return fd, fp.T, schur


def solution(mesh):
    return jax.shard_map(
        per_device,
        mesh=mesh,
        in_specs=(P(("row", "col"), None), P("row", "col"), P("row", "col")),
        out_specs=(P(("row", "col"), None), P("row", "col"), P("row", "col")),
        check_vma=False,
    )
```

```python
import functools

import jax
import jax.numpy as jnp
from jax import lax
from jax.experimental import pallas as pl
from jax.experimental.pallas import tpu as pltpu
from jax.sharding import PartitionSpec as P

NB = 512
F32 = jnp.float32
BF16 = jnp.bfloat16
MESH = pl.DeviceIdType.MESH
CHIPS = 16
COLS = 8


def split(x):
    high = x.astype(BF16)
    return high, (x - high.astype(F32)).astype(BF16)


def mm(a, b, dims):
    return lax.dot_general(a, b, (dims, ((), ())), preferred_element_type=F32)


NN = ((1,), (0,))
NT = ((1,), (1,))


def dot3s(a, b, dims=NN):
    return mm(a[0], b[0], dims) + (mm(a[0], b[1], dims) + mm(a[1], b[0], dims))


def dot3(a, b, dims=NN):
    return dot3s(split(a), split(b), dims)


def dotp(a, b):
    bh, bl = split(b)
    w = jnp.concatenate([bh, bl], 1)
    out = mm(jnp.concatenate(split(a), 1), jnp.concatenate([w, w], 0), NN)
    n = b.shape[1]
    return out[:, :n] + out[:, n:]


def dotp_t(a, b):
    bh, bl = split(b)
    w = jnp.concatenate([jnp.concatenate([bh, bh], 1), jnp.concatenate([bl, bl], 1)], 0)
    out = mm(jnp.concatenate(split(a), 1), w, NT)
    n = b.shape[0]
    return out[:, :n] + out[:, n:]


def scales(top, tol):
    e = (top - 1.0) / (top + 1.0)
    out = []
    while e > tol:
        m = 2.0 / (2.0 - e * e)
        out.append((m, e))
        e = e * e * m / 2.0
    return 2.0 / (1.0 + top), out


def grid2(n):
    i = lax.broadcasted_iota(jnp.int32, (n, n), 0)
    j = lax.broadcasted_iota(jnp.int32, (n, n), 1)
    return i, j


TOL = {256: 3e-4, 128: 1e-3, 64: 1e-3, 32: 1e-3, 16: 1e-3}
SMALL = 0.15
BASE = 32
GROUP = 4


def half_split(m, n, dot, dot_t):
    i, j = grid2(n)
    one = jnp.where(i == j, 1.0, 0.0)
    start, steps = scales(1.0 + n, TOL[n])
    zs = [start * x[:, :n] for x in m]
    for k, (s, e) in enumerate(steps):
        if e < SMALL:
            ns = [(s * (one - z[:n])).astype(BF16) for z in zs]
        else:
            ns = [(2.0 * s) * one - s * z[:n] for z in zs]
        if k == len(steps) - 1:
            zs = [z[n:] for z in zs]
        if e < SMALL:
            zs = [s * z + mm(z.astype(BF16), nn, NN) for z, nn in zip(zs, ns)]
        else:
            zs = [dot(z, nn) for z, nn in zip(zs, ns)]
    return zs, [x[n:, n:] - dot_t(z, x[n:, :n]) for x, z in zip(m, zs)]


def high_low(z, first):
    high = z.astype(BF16).astype(F32)
    out = jnp.where(first, high, z - high).astype(BF16)
    return jnp.concatenate([out, out], 1)


def twice(n, b):
    rows = []
    for k in range(0, 128, 2 * b):
        rows += [n[k:k + b]] * 2
    return jnp.concatenate(rows, 0)


def dot_pair(hl, n, b):
    high = n.astype(BF16).astype(F32)
    w = jnp.concatenate([twice(high, b).astype(BF16), twice(n - high, b).astype(BF16)], 0)
    return mm(hl, w, NN)


def tile_split(tiles, ts, b):
    i, j = grid2(128)
    bi, bj = i // b, j // b
    pair = i // (2 * b) == j // (2 * b)
    even = bi % 2 == 0
    first = bj % 2 == 0
    unit = jnp.where(jnp.logical_and(jnp.logical_and(pair, even), i % b == j % b), 1.0, 0.0)
    start, steps = scales(1.0 + b, TOL[b])
    doubled = [jnp.where(pair, jnp.where(first, m, pltpu.roll(m, b, 1)), 0.0) for m in tiles]
    zs = [start * d for d in doubled]
    for s, e in steps:
        if e < SMALL:
            ns = [jnp.where(even, s * (unit - z), 0.0).astype(BF16) for z in zs]
            zs = [s * z + mm(z.astype(BF16), nn, NN) for z, nn in zip(zs, ns)]
        else:
            ns = [(2.0 * s) * unit - s * z for z in zs]
            zs = [dot_pair(high_low(z, first), nn, b) for z, nn in zip(zs, ns)]
    gs = [high_low(jnp.where(even, 0.0, z), first) for z in zs]
    out = []
    for m, g, d in zip(tiles, gs, doubled):
        lows = split(jnp.where(even, 0.0, d))
        out.append(jnp.where(bi == bj, m, 0.0) - mm(g, jnp.concatenate(lows, 1), NT))
    if ts is None:
        g_only = [jnp.where(jnp.logical_and(first, jnp.logical_not(even)), z, 0.0) for z in zs]
        return out, [jnp.where(i == j, 1.0, 0.0) - g for g in g_only]
    return out, [t - dot_pair(g, t, b) for t, g in zip(ts, gs)]


def base_factors(tiles):
    sub = lax.broadcasted_iota(jnp.int32, (BASE, 128), 0)
    lane = lax.broadcasted_iota(jnp.int32, (BASE, 128), 1)
    groups = 128 // BASE
    rows = []
    for m in tiles:
        acc = None
        for g in range(groups):
            part = jnp.where(lane // BASE == g, m[g * BASE:(g + 1) * BASE], 0.0)
            acc = part if acc is None else acc + part
        rows.append(acc)
    ident = jnp.where(sub == lane % BASE, 1.0, 0.0)
    es = [ident] * len(tiles)
    for p0 in range(0, BASE, GROUP):
        index = [(lane // BASE) * BASE + p0 + c for c in range(GROUP)]
        for t in range(len(tiles)):
            cols = [jnp.take_along_axis(rows[t], i, axis=1, mode="promise_in_bounds")
                    for i in index]
            for c in range(GROUP):
                p = p0 + c
                root = lax.rsqrt(cols[c][p:p + 1])
                e_row = es[t][p:p + 1] * root
                if p == BASE - 1:
                    es[t] = jnp.where(sub == p, e_row, es[t])
                    break
                inv = root * root
                below = jnp.where(sub > p, cols[c], 0.0)
                for q in range(c + 1, GROUP):
                    cols[q] = cols[q] - below * (cols[q][p:p + 1] * inv)
                if p0 + GROUP < BASE:
                    rows[t] = rows[t] - below * (rows[t][p:p + 1] * inv)
                es[t] = jnp.where(sub == p, e_row, es[t] - below * (e_row * root))
    return [jnp.concatenate([jnp.where(lane // BASE == g, e, 0.0) for g in range(groups)], 0)
            for e in es]


def factor_inverse(a, between=lambda: None):
    (g1,), (s,) = half_split([a()], 256, dot3, lambda x, y: dot3(x, y, NT))
    blocks = [a()[:256, :256], s]
    g2, s2 = half_split(blocks, 128, dotp, dotp_t)
    tiles = [blocks[0][:128, :128], s2[0], blocks[1][:128, :128], s2[1]]
    ts = None
    b = 64
    while b >= BASE:
        tiles, ts = tile_split(tiles, ts, b)
        b //= 2
    g1p = jnp.concatenate([g1[:128], g1[128:] - dotp(g2[1], g1[:128])], 0)
    bases = base_factors(tiles)
    between()
    ts = [dotp(e, t) for e, t in zip(bases, ts)]
    zero = jnp.zeros((128, 128), F32)
    w11, w22 = [jnp.concatenate([
        jnp.concatenate([ts[2 * k], zero], 1),
        jnp.concatenate([-dotp(ts[2 * k + 1], g2[k]), ts[2 * k + 1]], 1)], 0) for k in range(2)]
    w21 = -jnp.concatenate([dotp(ts[2], g1p[:128]), dotp(ts[3], g1p[128:])], 0)

    i, j = grid2(256)
    one = jnp.where(i == j, 1.0, 0.0)
    low_half = jnp.where(i > j, 1.0, jnp.where(i == j, 0.5, 0.0))
    a_s = split(a())
    w1s = split(w11)
    w2s = split(jnp.concatenate([w21, w22], 1))
    wa1 = split(dot3s(w1s, [x[:256, :256] for x in a_s]))
    wa2 = split(dot3s(w2s, a_s))
    p11 = ((dot3s(wa1, w1s, NT) - one) * low_half).astype(BF16)
    p21 = dot3s([x[:, :256] for x in wa2], w1s, NT).astype(BF16)
    p22 = ((dot3s(wa2, w2s, NT) - one) * low_half).astype(BF16)
    n11 = w11 - mm(p11, w1s[0], NN)
    nw2 = mm(p22, w2s[0], NN)
    return n11, w21 - nw2[:, :256] - mm(p21, w1s[0], NN), w22 - nw2[:, 256:]


def step_kernel(d_ref, b_ref, t_ref, bc_ref, fd_ref, fp_ref, uh_ref, ul_ref, to_ref,
                g_ref, br_ref, m_ref, a4_ref, p_ref, bt_ref,
                az_s, az_r, ax_s, ax_r, ay_s, ay_r, ac_s, ac_r,
                bz_s, bz_r, mv_s, mv_r, bx_s, bx_r, by_s, by_r, bk_s, bk_r, loc_sem):
    row = lax.axis_index("row")
    z = lax.axis_index("col")
    chip = row // 2
    core = row % 2
    y = chip // 4
    x = chip % 4

    def at_z(k):
        return {"row": row, "col": (z + k) % COLS}

    def at_chip(k):
        return {"row": ((chip + k) % CHIPS) * 2 + core, "col": z}

    def at_x(k):
        return {"row": (y * 4 + (x + k) % 4) * 2 + core, "col": z}

    def at_y(k):
        return {"row": (((y + k) % 4) * 4 + x) * 2 + core, "col": z}

    partner = {"row": row + 1 - 2 * core, "col": z}

    def copy(src, dst, ssem, rsem, device):
        return pltpu.make_async_remote_copy(
            src_ref=src, dst_ref=dst, send_sem=ssem, recv_sem=rsem,
            device_id=device, device_id_type=MESH)

    def fan(ref, ssem, rsem, first, where, n):
        return [copy(ref, ref, ssem.at[first + k - 1], rsem.at[first + k - 1], where(k))
                for k in range(1, n + 1)]

    barrier = pltpu.get_barrier_semaphore()
    for k in (4, 3, 5, 2, 6, 1, 7):
        pl.semaphore_signal(barrier, inc=1, device_id=at_z(k), device_id_type=MESH)
    for k in (2, 1, 3):
        pl.semaphore_signal(barrier, inc=1, device_id=at_x(k), device_id_type=MESH)
        pl.semaphore_signal(barrier, inc=1, device_id=at_y(k), device_id_type=MESH)
    pl.semaphore_signal(barrier, inc=1, device_id=partner, device_id_type=MESH)

    @pl.when(z != 0)
    def _():
        for k in (2 * z, CHIPS - 2 * z):
            pl.semaphore_signal(barrier, inc=1, device_id=at_chip(k), device_id_type=MESH)

    own_tile = g_ref.at[y, x, core, z]
    own_a = pltpu.make_async_copy(d_ref, own_tile, loc_sem.at[0])
    own_b = pltpu.make_async_copy(b_ref, br_ref.at[z], loc_sem.at[1])
    own_t = pltpu.make_async_copy(t_ref, to_ref, loc_sem.at[4])
    own_a.start()
    own_b.start()
    pl.semaphore_wait(barrier, COLS + 6 + 2 * ((z + COLS - 1) // COLS))

    a_z = [copy(d_ref, own_tile, az_s.at[k - 1], az_r.at[k - 1], at_z(k))
           for k in range(1, COLS)]
    for k in (4, 3, 5, 2, 6, 1, 7):
        a_z[k - 1].start()

    move1 = copy(b_ref, m_ref, mv_s.at[0], mv_r.at[0], at_chip(2 * z))
    move1_own = pltpu.make_async_copy(b_ref, m_ref, loc_sem.at[2])

    @pl.when(z != 0)
    def _():
        move1.start()

    @pl.when(z == 0)
    def _():
        move1_own.start()

    own_t.start()
    own_a.wait()
    for c in a_z:
        c.wait()

    lo, hi = pl.ds(0, 4), pl.ds(4, 4)
    a_x = fan(g_ref.at[y, x, core, lo], ax_s, ax_r, 0, at_x, 3)
    a_y = fan(g_ref.at[y, x, core, hi], ay_s, ay_r, 0, at_y, 3)
    for k in (1, 0, 2):
        a_x[k].start()
        a_y[k].start()

    @pl.when(z != 0)
    def _():
        move1.wait()

    @pl.when(z == 0)
    def _():
        move1_own.wait()

    src = (chip + CHIPS - 2 * z) % CHIPS
    plane = src // 2
    slot = bc_ref.at[core, y, x]
    move2 = copy(m_ref, slot, mv_s.at[1], mv_r.at[1], {"row": row, "col": plane})
    move2_own = pltpu.make_async_copy(m_ref, slot, loc_sem.at[3])

    @pl.when(plane != z)
    def _():
        move2.start()

    @pl.when(plane == z)
    def _():
        move2_own.start()

    for c in a_x:
        c.wait()
    a_xy = fan(g_ref.at[y, :, core, lo], ay_s, ay_r, 3, at_y, 3)
    for k in (1, 0, 2):
        a_xy[k].start()
    for c in a_y:
        c.wait()
    a_yx = fan(g_ref.at[:, x, core, hi], ax_s, ax_r, 3, at_x, 3)
    for k in (1, 0, 2):
        a_yx[k].start()

    def to_partner(ref, ssem, rsem, k):
        c = copy(ref, ref, ssem.at[k], rsem.at[k], partner)
        c.start()
        return c

    a_c = [to_partner(g_ref.at[y, :, core, lo], ac_s, ac_r, 0),
           to_partner(g_ref.at[:, x, core, hi], ac_s, ac_r, 4)]

    @pl.when(plane != z)
    def _():
        move2.wait()

    @pl.when(plane == z)
    def _():
        move2_own.wait()

    blo, bhi = pl.ds(0, 32), pl.ds(32, 32)
    b_x = fan(bc_ref.at[core, y, x, blo], bx_s, bx_r, 0, at_x, 3)
    b_y = fan(bc_ref.at[core, y, x, bhi], by_s, by_r, 0, at_y, 3)
    for p, q in zip(b_x, b_y):
        p.start()
        q.start()

    b_z = [copy(b_ref, br_ref.at[z], bz_s.at[k - 1], bz_r.at[k - 1], at_z(k))
           for k in range(1, COLS)]
    for c in b_z:
        c.start()

    for k in range(1, 4):
        a_xy[k - 1].wait_recv()
        a_c.append(to_partner(g_ref.at[(y + 4 - k) % 4, :, core, lo], ac_s, ac_r, k))
        a_yx[k - 1].wait_recv()
        a_c.append(to_partner(g_ref.at[:, (x + 4 - k) % 4, core, hi], ac_s, ac_r, 4 + k))
    for c in a_xy + a_yx:
        c.wait_send()

    for c in b_x:
        c.wait()
    b_xy = fan(bc_ref.at[core, y, :, blo], by_s, by_r, 3, at_y, 3)
    for c in b_xy:
        c.start()
    for c in b_y:
        c.wait()
    b_yx = fan(bc_ref.at[core, :, x, bhi], bx_s, bx_r, 3, at_x, 3)
    for c in b_yx:
        c.start()
    def place(k):
        for c in range(CHIPS):
            for s in range(2):
                for l in range(4):
                    a4_ref[l, pl.ds(32 * c + 16 * k + s, 8, stride=2), :] = (
                        g_ref[c // 4, c % 4, k, :, 2 * l + s, :])

    place(core)
    for c in a_c:
        c.wait()
    place(1 - core)

    def block():
        return jnp.concatenate([a4_ref[l] for l in range(4)], 1)

    b_c = []

    def between():
        b_c.append(to_partner(bc_ref.at[core, y, :, blo], bk_s, bk_r, 0))
        b_c.append(to_partner(bc_ref.at[core, :, x, bhi], bk_s, bk_r, 4))
        own_b.wait()
        for c in b_z:
            c.wait()
        bt_ref[...] = br_ref[...].reshape(512, 256).T
        for k in range(1, 4):
            b_xy[k - 1].wait()
            b_c.append(to_partner(bc_ref.at[core, (y + 4 - k) % 4, :, blo], bk_s, bk_r, k))
            b_yx[k - 1].wait()
            b_c.append(to_partner(bc_ref.at[core, :, (x + 4 - k) % 4, bhi], bk_s, bk_r, 4 + k))

    w11, w21, w22 = factor_inverse(block, between)
    w1s = split(w11)
    w2s = split(jnp.concatenate([w21, w22], 1))
    d = row * COLS + z
    sixteen = pl.ds(pl.multiple_of((d // 8) * 16, 16), 16)
    mine = split(jnp.concatenate([a4_ref[l, sixteen, :] for l in range(4)], 1))
    b_s = [jnp.concatenate(v, 0) for v in zip(split(bt_ref[...]), mine)]
    p1 = dot3s([v[:, :256] for v in b_s], w1s, NT)
    p2 = dot3s(b_s, w2s, NT)
    p_ref[:, 0:256] = p1
    p_ref[:, 256:512] = p2
    p2s = split(p2[:256])
    u2 = dot3s(p2s, w2s)
    u1 = u2[:, :256] + dot3s(split(p1[:256]), w1s)
    for cols, u in ((slice(0, 256), u1), (slice(256, 512), u2[:, 256:])):
        uh_ref[:, cols], ul_ref[:, cols] = split(u)
    lane = lax.broadcasted_iota(jnp.int32, (1, 512), 1)
    for s in range(2):
        line_s = p_ref[pl.ds(256 + 2 * (d % 8) + s, 1), :]
        line_s = jnp.where(lane <= 2 * d + s, line_s, 0.0)
        for l in range(4):
            fd_ref[2 * l + s:2 * l + s + 1, :] = line_s[:, l * 128:(l + 1) * 128]
    part = p_ref[0:256, pl.ds(pl.multiple_of((z // 2) * 128, 128), 128)].T
    fp_ref[...] = jnp.where(z % 2 == 0, part[:64], part[64:])
    own_t.wait()
    for c in b_c:
        c.wait()


def step(d_tile, b_t, trailing):
    vmem = pl.BlockSpec(memory_space=pltpu.VMEM)
    hbm = pl.BlockSpec(memory_space=pltpu.HBM)
    dma = lambda n: [pltpu.SemaphoreType.DMA((n,))] * 2
    return pl.pallas_call(
        step_kernel,
        out_shape=(
            jax.ShapeDtypeStruct((2, 4, 4, 64, 256), F32),
            jax.ShapeDtypeStruct((8, 128), F32),
            jax.ShapeDtypeStruct((64, 256), F32),
            jax.ShapeDtypeStruct((256, 512), BF16),
            jax.ShapeDtypeStruct((256, 512), BF16),
            jax.ShapeDtypeStruct((256, 1024), F32),
        ),
        in_specs=[hbm] * 3,
        out_specs=(vmem,) * 6,
        scratch_shapes=[
            pltpu.VMEM((4, 4, 2, COLS, 8, 128), F32),
            pltpu.VMEM((COLS, 64, 256), F32),
            pltpu.VMEM((64, 256), F32),
            pltpu.VMEM((4, 512, 128), F32),
            pltpu.VMEM((272, 512), F32),
            pltpu.VMEM((256, 512), F32),
            *dma(7), *dma(6), *dma(6), *dma(8),
            *dma(7), *dma(2), *dma(6), *dma(6), *dma(8),
            pltpu.SemaphoreType.DMA((5,)),
        ],
        compiler_params=pltpu.CompilerParams(
            collective_id=0, has_side_effects=True, vmem_limit_bytes=40 * 1024 * 1024),
        name="step",
    )(*[pltpu.with_memory_space_constraint(v, pltpu.HBM) for v in (d_tile, b_t, trailing)])


def update_kernel(uh_ref, ul_ref, bc_ref, t_ref, fd_in, fp_in, s_ref, fd_ref, fp_ref,
                  out_ref, sem):
    z = lax.axis_index("col")
    u_s = (uh_ref[...], ul_ref[...])
    copies = []
    for q in range(4):
        b, core = q // 2, q % 2
        rows = jnp.concatenate([bc_ref[core, (k + z) % COLS, b] for k in range(COLS)], 0)
        cols = slice(q * 256, (q + 1) * 256)
        out_ref[q] = t_ref[:, cols] - dot3s(u_s, split(rows))
        copies.append(pltpu.make_async_copy(out_ref.at[q], s_ref.at[:, cols], sem.at[q]))
        copies[-1].start()
    fd_ref[...] = fd_in[...]
    fp_ref[...] = fp_in[...]
    for c in copies:
        c.wait()


def update(uh, ul, bc, trailing, fd, fp):
    vmem = pl.BlockSpec(memory_space=pltpu.VMEM)
    return pl.pallas_call(
        update_kernel,
        out_shape=(
            jax.ShapeDtypeStruct((256, 1024), F32),
            jax.ShapeDtypeStruct((8, 128), F32),
            jax.ShapeDtypeStruct((64, 256), F32),
        ),
        in_specs=[vmem] * 6,
        out_specs=(pl.BlockSpec(memory_space=pltpu.HBM), vmem, vmem),
        scratch_shapes=[pltpu.VMEM((4, 256, 256), F32), pltpu.SemaphoreType.DMA((4,))],
        compiler_params=pltpu.CompilerParams(vmem_limit_bytes=16 * 1024 * 1024),
        name="update",
    )(uh, ul, bc, trailing, fd, fp)


def per_device(diag_block, panel_block, trailing):
    tile = diag_block.reshape(2, 4, 128).transpose(1, 0, 2).reshape(8, 128)
    bc, fd, fp, uh, ul, t = step(tile, panel_block.T, trailing)
    schur, fd, fp = update(uh, ul, bc.reshape(2, COLS, 2, 64, 256), t, fd, fp)
    fd = fd.reshape(4, 2, 128).transpose(1, 0, 2).reshape(2, 512)
    return fd, fp.T, schur


def solution(mesh):
    return jax.shard_map(
        per_device,
        mesh=mesh,
        in_specs=(P(("row", "col"), None), P("row", "col"), P("row", "col")),
        out_specs=(P(("row", "col"), None), P("row", "col"), P("row", "col")),
        check_vma=False,
    )
```
